128 devices in a mesh: grp: 4 (over y), own: 32 (over x, z, core).
Axes of the slice: x: 4, y: 4, z: 4, core: 2. Of those that a mesh axis runs over, the one named last changes fastest.
Arguments:
- embeddings: float32 [98304, 768], P(('grp', 'own')), may hold values from -64 to 64
- cluster_ids: int32 [98304], P(('grp', 'own')), may hold values from 0 to 511, as said below
- owner_map: int32 [512], replicated, may hold values from 0 to 31, as said below
- source_order: int32 [98304], P(('grp', 'own')), may hold values from 0 to 767, as said below
Outputs:
- dup_score: float32 [98304], P(('grp', 'own'))
- centroids: float32 [512, 768], P('own')
The draws below stay inside these ranges and needn't reach their ends.
Inputs may be any that keep to these rules, and one draw needn't show every extreme that they name: `owner_map`: every owner index is given to exactly 16 clusters. `cluster_ids`: within the 768 rows of one device, at most 48 rows have clusters of one owner index; in every draw some owner index receives exactly 48 rows from every device, and every device sends exactly 48 rows to some owner index. Cluster sizes are uneven and some clusters may be empty. `source_order`: each aligned block of 768 entries is a permutation of 0 to 767.
All inputs are finite; a program needn't handle non-finite values.
Results may differ from the reference program's by a relative error of at most 0.0003.
Values sent between devices are 32-bit elements; how exact they have to be, the bound alone decides.
A program may use at most 128 MiB of HBM per device.

```python
import jax
import jax.numpy as jnp
from jax import lax

D = 768
R_DEV = 768
CL_OWN = 16
CLUSTERS = 512
CAP = 48
ROWS = 98304
N_GRP = 4
N_OWN = 32


def layout(base_key):
    owner_total = CLUSTERS // CL_OWN
    block_total = ROWS // R_DEV
    slot_total = owner_total * CAP
    cluster_perm = jax.random.permutation(jax.random.fold_in(base_key, 11), CLUSTERS).astype(jnp.int32)
    owner_map = (cluster_perm // CL_OWN).astype(jnp.int32)
    owned_cluster = jnp.argsort(cluster_perm).astype(jnp.int32)
    hot_owner = jax.random.randint(jax.random.fold_in(base_key, 12), (), 0, owner_total)
    base_bias = jax.random.randint(jax.random.fold_in(base_key, 13), (owner_total,), 0, 4)
    owner_index = jnp.arange(owner_total, dtype=jnp.int32)
    slot_owner = jnp.arange(slot_total, dtype=jnp.int32) // CAP

    def one_block(block_key):
        forced = jax.random.randint(jax.random.fold_in(block_key, 1), (), 0, owner_total)
        extra_bias = jax.random.randint(jax.random.fold_in(block_key, 2), (owner_total,), 0, 2)
        owner_bias = jnp.where(owner_index == forced, -2, base_bias + extra_bias)
        owner_bias = jnp.where(owner_index == hot_owner, -3, owner_bias)
        slot_perm = jax.random.permutation(jax.random.fold_in(block_key, 3), slot_total).astype(jnp.int32)
        slot_score = owner_bias[slot_owner] * slot_total + slot_perm
        chosen = jnp.argsort(slot_score)[:R_DEV]
        row_perm = jax.random.permutation(jax.random.fold_in(block_key, 4), R_DEV)
        row_owner = slot_owner[chosen][row_perm]
        upper_bound = jax.random.randint(jax.random.fold_in(block_key, 5), (R_DEV,), 1, CL_OWN + 1)
        local_index = jax.random.randint(jax.random.fold_in(block_key, 6), (R_DEV,), 0, upper_bound)
        return owned_cluster[row_owner * CL_OWN + local_index]
    block_keys = jax.random.split(jax.random.fold_in(base_key, 14), block_total)
    cluster_ids = lax.map(one_block, block_keys).reshape(ROWS).astype(jnp.int32)
    return (owner_map, cluster_ids)


def draw_owner_map(key, part):
    return layout(key)[0]


def draw_cluster_ids(key, part):
    return layout(key)[1]


def draw_embeddings(key, part):
    owner_map, cluster_ids = layout(key)
    direction_count = 16
    base_count = 8
    centers = jnp.clip(jax.random.normal(jax.random.fold_in(key, 21), (CLUSTERS, D), jnp.float32), -4.0, 4.0)
    directions = jnp.clip(jax.random.normal(jax.random.fold_in(key, 25), (CLUSTERS, direction_count, D), jnp.float32), -4.0, 4.0)
    pick_first = jax.random.randint(jax.random.fold_in(key, 26), (ROWS,), 0, direction_count)
    pick_second = jax.random.randint(jax.random.fold_in(key, 27), (ROWS,), 0, direction_count)
    mix_weights = jax.random.uniform(jax.random.fold_in(key, 28), (ROWS, 2), jnp.float32, 0.3, 1.5)
    sub_part = mix_weights[:, 0:1] * directions[cluster_ids, pick_first] + mix_weights[:, 1:2] * directions[cluster_ids, pick_second]
    strength = jnp.exp(jax.random.uniform(jax.random.fold_in(key, 23), (ROWS, 1), jnp.float32, jnp.log(0.3), jnp.log(3.0)))
    copy_bases = jnp.clip(jax.random.normal(jax.random.fold_in(key, 29), (CLUSTERS, base_count, D), jnp.float32), -4.0, 4.0)
    copy_pick = jax.random.randint(jax.random.fold_in(key, 30), (ROWS,), 0, base_count)
    copy_flag = jax.random.uniform(jax.random.fold_in(key, 31), (ROWS, 1), jnp.float32) < 0.15
    jitter_level = jax.random.uniform(jax.random.fold_in(key, 32), (ROWS, 1), jnp.float32, 0.1, 0.33)
    noise_part = jnp.clip(jax.random.normal(jax.random.fold_in(key, 22), (ROWS, D), jnp.float32), -4.0, 4.0)
    main_row = strength * centers[cluster_ids] + sub_part + noise_part
    copy_row = centers[cluster_ids] + copy_bases[cluster_ids, copy_pick] + 1.41421356 * jitter_level * noise_part
    chosen_row = jnp.where(copy_flag, copy_row, main_row)
    return jnp.clip(chosen_row, -64.0, 64.0)


def block_order(block_key):
    return jax.random.permutation(block_key, R_DEV).astype(jnp.int32)


def draw_source_order(key, part):
    block_keys = jax.random.split(jax.random.fold_in(key, 31), ROWS // R_DEV)
    return lax.map(block_order, block_keys).reshape(ROWS)


def setup_inputs(seed: int = 0) -> dict:
    key_list = jax.random.split(jax.random.key(seed), 5)
    embeddings = draw_embeddings(jax.random.fold_in(key_list[4], 71), 0)
    cluster_ids = draw_cluster_ids(jax.random.fold_in(key_list[4], 71), 0)
    owner_map = draw_owner_map(jax.random.fold_in(key_list[4], 71), 0)
    source_order = draw_source_order(jax.random.fold_in(key_list[4], 71), 0)
    return {"embeddings": embeddings, "cluster_ids": cluster_ids, "owner_map": owner_map, "source_order": source_order}


sharpness = 6.0

def unit_rows(embeddings):
    squares = lax.optimization_barrier(jnp.sum(embeddings * embeddings, axis=1, keepdims=True))
    return embeddings * lax.rsqrt(squares + 1e-06)

def owner_positions(owner_map):
    cluster_index = jnp.arange(owner_map.shape[0], dtype=jnp.int32)
    same_owner = owner_map[:, None] == owner_map[None, :]
    earlier = cluster_index[None, :] < cluster_index[:, None]
    before = lax.optimization_barrier(jnp.sum((same_owner & earlier).astype(jnp.int32), axis=1)).astype(jnp.int32)
    return (owner_map * CL_OWN + before).astype(jnp.int32)

def owner_mass(owner_pair):
    owner_rows, owner_ids = owner_pair
    pool_count = owner_rows.shape[0]
    block_rows = 512 if pool_count % 512 == 0 else pool_count
    right_rows = owner_rows
    left_blocks = right_rows.reshape(pool_count // block_rows, block_rows, right_rows.shape[1])
    left_ids = owner_ids.reshape(pool_count // block_rows, block_rows)

    def one_block(block_pair):
        scores = jnp.dot(block_pair[0], right_rows.T, precision=lax.Precision.HIGHEST)
        linked = (block_pair[1][:, None] == owner_ids[None, :]) & (block_pair[1][:, None] >= 0)
        return lax.optimization_barrier(jnp.sum(jnp.where(linked, jnp.exp(sharpness * (scores - 1.0)), 0.0), axis=1))
    return lax.map(one_block, (left_blocks, left_ids)).reshape(pool_count)

def reference(embeddings, cluster_ids, owner_map, source_order):
    device_total = N_GRP * N_OWN
    unit_embed = unit_rows(embeddings)
    row_owner = owner_map[cluster_ids].astype(jnp.int32)
    owner_hot = (row_owner.reshape(device_total, R_DEV)[:, :, None] == jnp.arange(N_OWN, dtype=jnp.int32)[None, None, :]).astype(jnp.int32)
    rank_index = (lax.optimization_barrier(jnp.sum(jnp.cumsum(owner_hot, axis=1) * owner_hot, axis=2)) - 1).reshape(ROWS).astype(jnp.int32)
    source_index = (jnp.arange(ROWS, dtype=jnp.int32) // R_DEV).astype(jnp.int32)
    column_index = (source_index * CAP + rank_index).astype(jnp.int32)
    pool_count = device_total * CAP
    owner_rows = jnp.zeros((N_OWN, pool_count, D), unit_embed.dtype).at[row_owner, column_index].set(unit_embed)
    owner_ids = jnp.full((N_OWN, pool_count), -1, jnp.int32).at[row_owner, column_index].set(cluster_ids)
    dup_mass = lax.map(owner_mass, (owner_rows, owner_ids))
    row_score = jnp.log(dup_mass[row_owner, column_index])
    target_index = (source_index * R_DEV + source_order).astype(jnp.int32)
    dup_score = jnp.zeros((ROWS,), jnp.float32).at[target_index].set(row_score)
    position = owner_positions(owner_map)
    cluster_sums = jax.ops.segment_sum(unit_embed, position[cluster_ids], num_segments=CLUSTERS)
    centroids = cluster_sums * lax.rsqrt(lax.optimization_barrier(jnp.mean(cluster_sums * cluster_sums, axis=1, keepdims=True)) + 1e-06)
    return (dup_score, centroids)
```

```python
import functools

import jax
import jax.numpy as jnp
from jax import lax
from jax.experimental import pallas as pl
from jax.experimental.pallas import tpu as pltpu
from jax.sharding import PartitionSpec as P

MESH = pl.DeviceIdType.MESH
F32 = jnp.float32
BF16 = jnp.bfloat16

N_GRP = 4
N_OWN = 32
D = 768
R_DEV = 768
CLUSTERS = 512
CL_OWN = 16
CAP = 48
SLOTS = N_OWN * CAP
MSGS = N_GRP * N_OWN
STEP = 13
CHUNK_MSGS = 16
CHUNK = CHUNK_MSGS * CAP
CHUNKS = MSGS // CHUNK_MSGS
SHARPNESS = 6.0


def hot(condition):
    return jnp.where(condition, 1.0, 0.0).astype(BF16)


def iota(shape, dim):
    return lax.broadcasted_iota(jnp.int32, shape, dim)


def by_48(n):
    return (n * 1366) >> 16


def dot(a, b):
    return lax.dot_general(a, b, (((1,), (0,)), ((), ())), preferred_element_type=F32)


def dot_t(a, b):
    return lax.dot_general(a, b, (((1,), (1,)), ((), ())), preferred_element_type=F32)


def split3(a):
    high = a.astype(BF16)
    rest = a - high.astype(F32)
    middle = rest.astype(BF16)
    low = (rest - middle.astype(F32)).astype(BF16)
    return high, middle, low


def exact(product, a, b):
    high, middle, low = split3(a)
    return product(high, b) + (product(middle, b) + product(low, b))


def home_row(owner):
    x, z, core = owner // 8, lax.rem(owner // 2, 4), lax.rem(owner, 2)
    return lax.rem(x + z, 2) + 2 * core


def kernel(
    x_ref, cid_ref, map_ref, order_ref, dup_ref, cen_ref,
    packed, ids_out, land, ids_in, unit, row_acc, col_acc, id_col, id_row, sums, rowhot_ref, rank_ref,
    mass_out, mass_in, cen_in,
    send_sem, ids_send_sem, recv_sem, ids_recv_sem, local_sem, back_send_sem, back_recv_sem, cen_send_sem, cen_recv_sem,
):
    me, grp = lax.axis_index("own"), lax.axis_index("grp")
    home = grp == home_row(me)

    owner_hot = hot(iota((N_OWN, CLUSTERS), 0) == map_ref[...])
    earlier = hot(iota((CLUSTERS, CLUSTERS), 0) < iota((CLUSTERS, CLUSTERS), 1))
    before = dot(owner_hot, earlier)
    place = jnp.sum(owner_hot.astype(F32) * before, axis=0, keepdims=True)
    table = jnp.concatenate([owner_hot, jnp.broadcast_to(place, (16, CLUSTERS)).astype(BF16)], axis=0)
    looked_up = dot(table, hot(iota((CLUSTERS, R_DEV), 0) == cid_ref[...]))
    row_hot, row_place = looked_up[:N_OWN], looked_up[N_OWN : N_OWN + 1]
    ahead = hot(iota((R_DEV, R_DEV), 0) < iota((R_DEV, R_DEV), 1))
    rank = jnp.sum(row_hot * dot(row_hot.astype(BF16), ahead), axis=0, keepdims=True)
    owner = jnp.sum(row_hot * iota((N_OWN, R_DEV), 0).astype(F32), axis=0, keepdims=True)
    rank = rank.astype(jnp.int32)
    slot = owner.astype(jnp.int32) * CAP + rank
    rank_hot = hot(iota((128, R_DEV), 0) == rank)
    rowhot_ref[...] = row_hot
    rank_ref[...] = rank_hot
    ids = dot_t((row_hot * (row_place + 1.0)).astype(BF16), rank_hot) - 1.0
    for o in range(N_OWN):
        ids_out[o] = jnp.broadcast_to(ids[o : o + 1], (8, 128))

    x = x_ref[...]
    u = x * lax.rsqrt(jnp.sum(x * x, axis=1, keepdims=True) + 1e-06)
    high = u.astype(BF16)
    low = (u - high.astype(F32)).astype(BF16)
    block = SLOTS // 4
    for k in range(4):
        pick = hot(iota((block, R_DEV), 0) + k * block == slot)
        packed[pl.ds(k * block, block)] = dot(pick, high) + dot(pick, low)

    def send(i, _):
        o = lax.rem(me + lax.rem(STEP * i, N_OWN), N_OWN)
        to = home_row(o)
        here = (o == me) & (to == grp)
        start = pl.multiple_of(o * CAP, CAP)
        m = i * N_GRP + grp
        stop = pl.multiple_of(m * CAP, CAP)

        @pl.when(jnp.logical_not(here))
        def _():
            pltpu.make_async_remote_copy(
                src_ref=ids_out.at[o], dst_ref=ids_in.at[m], send_sem=ids_send_sem,
                recv_sem=ids_recv_sem.at[i // N_GRP], device_id=(to, o), device_id_type=MESH,
            ).start()
            pltpu.make_async_remote_copy(
                src_ref=packed.at[pl.ds(start, CAP)], dst_ref=land.at[pl.ds(stop, CAP)], send_sem=send_sem,
                recv_sem=recv_sem.at[i // N_GRP], device_id=(to, o), device_id_type=MESH,
            ).start()

        @pl.when(here)
        def _():
            pltpu.make_async_copy(ids_out.at[o], ids_in.at[m], local_sem.at[0]).start()
            pltpu.make_async_copy(packed.at[pl.ds(start, CAP)], land.at[pl.ds(stop, CAP)], local_sem.at[1]).start()

        return 0

    lax.fori_loop(0, N_OWN, send, 0)

    def wait(ref, count, sem):
        pltpu.make_async_copy(ref.at[pl.ds(0, count)], ref.at[pl.ds(0, count)], sem).wait()

    cols = iota((128, CHUNK), 1)
    spread = hot(cols - CAP * by_48(cols) == iota((128, CHUNK), 0))
    mine = by_48(iota((CHUNK_MSGS, CHUNK), 1)) == iota((CHUNK_MSGS, CHUNK), 0)

    def pair(a, b, diagonal):
        left = pl.multiple_of(a * CHUNK, CHUNK)
        right = pl.multiple_of(b * CHUNK, CHUNK)
        part = 256
        cols_sum = [jnp.zeros((8, 128), F32)] * (CHUNK // 128)
        for r in range(CHUNK // part):
            rows = pl.ds(left + r * part, part)
            scores = dot_t(unit[rows], unit[pl.ds(right, CHUNK)])
            left_ids = id_col[rows]
            total = row_acc[rows]
            for t in range(CHUNK // 128):
                weights = jnp.exp(SHARPNESS * scores[:, t * 128 : (t + 1) * 128] - SHARPNESS)
                same = left_ids == id_row[0:1, pl.ds(right + t * 128, 128)]
                weights = jnp.where(same, weights, 0.0)
                total = total + weights
                if not diagonal:
                    cols_sum[t] = cols_sum[t] + jnp.sum(weights.reshape(part // 8, 8, 128), axis=0)
            row_acc[rows] = total
        if not diagonal:
            for t in range(CHUNK // 128):
                col_acc[:, pl.ds(right + t * 128, 128)] += cols_sum[t]

    @pl.when(home)
    def _():
        sums[...] = jnp.zeros_like(sums)
        row_acc[...] = jnp.zeros_like(row_acc)
        col_acc[...] = jnp.zeros_like(col_acc)
        wait(ids_out, 1, local_sem.at[0])
        pltpu.make_async_copy(packed.at[pl.ds(0, CAP)], packed.at[pl.ds(0, CAP)], local_sem.at[1]).wait()

        def chunk(a, _):
            @pl.when(a == 0)
            def _():
                wait(ids_in, CHUNK_MSGS - 1, ids_recv_sem.at[0])
                wait(land, CHUNK - CAP, recv_sem.at[0])

            @pl.when(a > 0)
            def _():
                wait(ids_in, CHUNK_MSGS, ids_recv_sem.at[a])
                wait(land, CHUNK, recv_sem.at[a])

            base = pl.multiple_of(a * CHUNK, CHUNK)
            rows = pl.ds(base, CHUNK)
            got = land[rows]
            high = got.astype(BF16)
            unit[rows] = high
            low = (got - high.astype(F32)).astype(BF16)
            ids = ids_in[pl.ds(a * CHUNK_MSGS, CHUNK_MSGS), 0, :].astype(BF16)
            in_row = jnp.where(mine, dot(ids, spread), 0.0).astype(BF16)
            row = dot(jnp.ones((8, CHUNK_MSGS), BF16), in_row)
            id_row[:, rows] = row
            at = iota((CHUNK, 128), 0)
            picked = dot(hot(by_48(iota((CHUNK, CHUNK_MSGS), 0)) == iota((CHUNK, CHUNK_MSGS), 1)), ids)
            picked = jnp.where(at - CAP * by_48(at) == iota((CHUNK, 128), 1), picked, 0.0).astype(BF16)
            id_col[rows] = dot(picked, jnp.ones((128, 128), BF16))
            member = hot(iota((CL_OWN, CHUNK), 0).astype(F32) == row[0:1])
            sums[...] += dot(member, high) + dot(member, low)
            lax.fori_loop(0, a, lambda b, _: (pair(a, b, False), 0)[1], 0)
            pair(a, a, True)
            return 0

        lax.fori_loop(0, CHUNKS, chunk, 0)

        def give_back(a, _):
            rows = pl.ds(pl.multiple_of(a * CHUNK, CHUNK), CHUNK)
            part = row_acc[rows]
            high, middle, low = split3(part)
            ones = jnp.ones((8, 128), BF16)
            mass = dot_t(ones, high) + (dot_t(ones, middle) + dot_t(ones, low))
            mass = mass[0:1] + jnp.sum(col_acc[:, rows], axis=0, keepdims=True)
            back = exact(dot_t, jnp.where(mine, mass, 0.0), spread)
            for j in range(CHUNK_MSGS):
                mass_out[a * CHUNK_MSGS + j] = jnp.broadcast_to(back[j : j + 1], (8, 128))
            for j in range(CHUNK_MSGS):
                i = a * (CHUNK_MSGS // N_GRP) + j // N_GRP
                to_grp = j % N_GRP
                to = lax.rem(me + N_OWN - lax.rem(STEP * i, N_OWN), N_OWN)
                here = (to == me) & (grp == to_grp)

                @pl.when(jnp.logical_not(here))
                def _():
                    pltpu.make_async_remote_copy(
                        src_ref=mass_out.at[a * CHUNK_MSGS + j], dst_ref=mass_in.at[me], send_sem=back_send_sem,
                        recv_sem=back_recv_sem, device_id=(to_grp, to), device_id_type=MESH,
                    ).start()

                @pl.when(here)
                def _():
                    pltpu.make_async_copy(mass_out.at[a * CHUNK_MSGS + j], mass_in.at[me], local_sem.at[2]).start()

            return 0

        lax.fori_loop(0, CHUNKS, give_back, 0)

        total = sums[...]
        cen_ref[...] = total * lax.rsqrt(jnp.mean(total * total, axis=1, keepdims=True) + 1e-06)
        for k in range(1, N_GRP):
            pltpu.make_async_remote_copy(
                src_ref=cen_ref, dst_ref=cen_in, send_sem=cen_send_sem.at[k - 1], recv_sem=cen_recv_sem,
                device_id=(lax.rem(grp + k, N_GRP), me), device_id_type=MESH,
            ).start()
        for k in range(1, N_GRP):
            pltpu.make_async_copy(cen_ref, cen_ref, cen_send_sem.at[k - 1]).wait()
        wait(mass_out, MSGS - 1, back_send_sem)
        wait(mass_out, 1, local_sem.at[2])
        wait(mass_in, N_OWN - 1, back_recv_sem)
        wait(packed, SLOTS - CAP, send_sem)
        wait(ids_out, N_OWN - 1, ids_send_sem)

    @pl.when(jnp.logical_not(home))
    def _():
        pltpu.make_async_copy(cen_in, cen_in, cen_recv_sem).wait()
        cen_ref[...] = cen_in[...]
        wait(mass_in, N_OWN, back_recv_sem)
        wait(packed, SLOTS, send_sem)
        wait(ids_out, N_OWN, ids_send_sem)

    got = exact(dot, mass_in[:, 0, :], rank_ref[...])
    mass = jnp.sum(got * rowhot_ref[...], axis=0, keepdims=True)
    score = jnp.broadcast_to(jnp.log(mass), (8, R_DEV))
    target = hot(iota((R_DEV, R_DEV), 0) == order_ref[...])
    dup_ref[...] = exact(dot_t, score, target)[0:1]


def local(embeddings, cluster_ids, owner_map, source_order):
    vmem = pl.BlockSpec(memory_space=pltpu.VMEM)
    dma = pltpu.SemaphoreType.DMA
    dup, centroids = pl.pallas_call(
        kernel,
        out_shape=(jax.ShapeDtypeStruct((1, R_DEV), F32), jax.ShapeDtypeStruct((CL_OWN, D), F32)),
        in_specs=[vmem] * 4,
        out_specs=(vmem, vmem),
        scratch_shapes=[
            pltpu.VMEM((SLOTS, D), F32),
            pltpu.VMEM((N_OWN, 8, 128), F32),
            pltpu.VMEM((MSGS * CAP, D), F32),
            pltpu.VMEM((MSGS, 8, 128), F32),
            pltpu.VMEM((MSGS * CAP, D), BF16),
            pltpu.VMEM((MSGS * CAP, 128), F32),
            pltpu.VMEM((8, MSGS * CAP), F32),
            pltpu.VMEM((MSGS * CAP, 128), F32),
            pltpu.VMEM((8, MSGS * CAP), F32),
            pltpu.VMEM((CL_OWN, D), F32),
            pltpu.VMEM((N_OWN, R_DEV), F32),
            pltpu.VMEM((128, R_DEV), BF16),
            pltpu.VMEM((MSGS, 8, 128), F32),
            pltpu.VMEM((N_OWN, 8, 128), F32),
            pltpu.VMEM((CL_OWN, D), F32),
            dma, dma, dma((CHUNKS,)), dma((CHUNKS,)), dma((3,)), dma, dma, dma((3,)), dma,
        ],
        compiler_params=pltpu.CompilerParams(has_side_effects=True, vmem_limit_bytes=60 << 20),
        name="owner_gather",
    )(
        embeddings,
        cluster_ids.reshape(1, R_DEV),
        owner_map.reshape(1, CLUSTERS),
        source_order.reshape(1, R_DEV),
    )
    return dup.reshape(R_DEV), centroids


def solution(mesh):
    placed = (P(("grp", "own"), None), P(("grp", "own")), P(), P(("grp", "own")))
    return jax.shard_map(
        local,
        mesh=mesh,
        in_specs=placed,
        out_specs=(P(("grp", "own")), P("own", None)),
        check_vma=False,
    )
```

```python
import functools

import jax
import jax.numpy as jnp
from jax import lax
from jax.experimental import pallas as pl
from jax.experimental.pallas import tpu as pltpu
from jax.sharding import PartitionSpec as P

MESH = pl.DeviceIdType.MESH
F32 = jnp.float32
BF16 = jnp.bfloat16

N_GRP = 4
N_OWN = 32
D = 768
R_DEV = 768
CLUSTERS = 512
CL_OWN = 16
CAP = 48
SLOTS = N_OWN * CAP
MSGS = N_GRP * N_OWN
STEP = 13
CHUNK_MSGS = 16
CHUNK = CHUNK_MSGS * CAP
CHUNKS = MSGS // CHUNK_MSGS
SHARPNESS = 6.0
WINDOW = 8
LAG = 6


def hot(condition):
    return jnp.where(condition, 1.0, 0.0).astype(BF16)


def iota(shape, dim):
    return lax.broadcasted_iota(jnp.int32, shape, dim)


def by_48(n):
    return (n * 1366) >> 16


def dot(a, b):
    return lax.dot_general(a, b, (((1,), (0,)), ((), ())), preferred_element_type=F32)


def dot_t(a, b):
    return lax.dot_general(a, b, (((1,), (1,)), ((), ())), preferred_element_type=F32)


def split3(a):
    high = a.astype(BF16)
    rest = a - high.astype(F32)
    middle = rest.astype(BF16)
    low = (rest - middle.astype(F32)).astype(BF16)
    return high, middle, low


def exact(product, a, b):
    high, middle, low = split3(a)
    return product(high, b) + (product(middle, b) + product(low, b))


def home_row(owner):
    x, z, core = owner // 8, lax.rem(owner // 2, 4), lax.rem(owner, 2)
    return lax.rem(x + z, 2) + 2 * core


def in_transit(source, grp, owner):
    z_step = lax.rem(owner // 2 - source // 2 + 2 * N_OWN, 4)
    y_step = lax.rem(home_row(owner) - grp + 4, 4)
    via = ((y_step == 1) & (z_step >= 2)) | ((y_step == 3) & (z_step >= 1) & (z_step <= 2))
    late = jnp.where(y_step == 1, z_step - 2, z_step - 1)
    return via, late * 8 + source // 8 * 2 + lax.rem(source, 2)


def kernel(
    x_ref, cid_ref, map_ref, order_ref, dup_ref, cen_ref,
    packed, ids_out, land, ids_in, unit, row_acc, col_acc, id_col, id_row, scale_col, scale_row, sums, rowhot_ref, rank_ref,
    mass_out, mass_in, cen_in, transit,
    send_sem, transit_sem, pass_sem, ids_send_sem, recv_sem, ids_recv_sem, local_sem, back_send_sem, back_recv_sem, cen_send_sem, cen_recv_sem,
):
    me, grp = lax.axis_index("own"), lax.axis_index("grp")
    home = grp == home_row(me)

    owner_hot = hot(iota((N_OWN, CLUSTERS), 0) == map_ref[...])
    earlier = hot(iota((CLUSTERS, CLUSTERS), 0) < iota((CLUSTERS, CLUSTERS), 1))
    before = dot(owner_hot, earlier)
    place = jnp.sum(owner_hot.astype(F32) * before, axis=0, keepdims=True)
    table = jnp.concatenate([owner_hot, jnp.broadcast_to(place, (16, CLUSTERS)).astype(BF16)], axis=0)
    looked_up = dot(table, hot(iota((CLUSTERS, R_DEV), 0) == cid_ref[...]))
    row_hot, row_place = looked_up[:N_OWN], looked_up[N_OWN : N_OWN + 1]
    ahead = hot(iota((R_DEV, R_DEV), 0) < iota((R_DEV, R_DEV), 1))
    rank = jnp.sum(row_hot * dot(row_hot.astype(BF16), ahead), axis=0, keepdims=True)
    owner = jnp.sum(row_hot * iota((N_OWN, R_DEV), 0).astype(F32), axis=0, keepdims=True)
    rank = rank.astype(jnp.int32)
    slot = owner.astype(jnp.int32) * CAP + rank
    rank_hot = hot(iota((128, R_DEV), 0) == rank)
    rowhot_ref[...] = row_hot
    rank_ref[...] = rank_hot
    ids = dot_t((row_hot * (row_place + 1.0)).astype(BF16), rank_hot) - 1.0
    for o in range(N_OWN):
        ids_out[o] = jnp.broadcast_to(ids[o : o + 1], (8, 128))

    x = x_ref[...]
    u = x * lax.rsqrt(jnp.sum(x * x, axis=1, keepdims=True) + 1e-06)
    high = u.astype(BF16)
    low = (u - high.astype(F32)).astype(BF16)
    block = SLOTS // 4
    for k in range(4):
        pick = hot(iota((block, R_DEV), 0) + k * block == slot)
        packed[pl.ds(k * block, block)] = dot(pick, high) + dot(pick, low)

    def at_slot(m):
        return pl.ds(pl.multiple_of(m * CAP, CAP), CAP)

    def send(i):
        o = lax.rem(me + lax.rem(STEP * i, N_OWN), N_OWN)
        to = home_row(o)
        here = (o == me) & (to == grp)
        via, place = in_transit(me, grp, o)
        m = i * N_GRP + grp

        @pl.when(jnp.logical_not(here))
        def _():
            pltpu.make_async_remote_copy(
                src_ref=ids_out.at[o], dst_ref=ids_in.at[m], send_sem=ids_send_sem,
                recv_sem=ids_recv_sem.at[i // N_GRP], device_id=(to, o), device_id_type=MESH,
            ).start()

        @pl.when(jnp.logical_not(here | via))
        def _():
            pltpu.make_async_remote_copy(
                src_ref=packed.at[at_slot(o)], dst_ref=land.at[at_slot(m)], send_sem=send_sem.at[i],
                recv_sem=recv_sem.at[i // N_GRP], device_id=(to, o), device_id_type=MESH,
            ).start()

        @pl.when(via)
        def _():
            pltpu.make_async_remote_copy(
                src_ref=packed.at[at_slot(o)], dst_ref=transit.at[at_slot(place)], send_sem=send_sem.at[i],
                recv_sem=transit_sem.at[i], device_id=(grp, o), device_id_type=MESH,
            ).start()

        @pl.when(here)
        def _():
            pltpu.make_async_copy(ids_out.at[o], ids_in.at[m], local_sem.at[0]).start()
            pltpu.make_async_copy(packed.at[at_slot(o)], land.at[at_slot(m)], send_sem.at[i]).start()

    def pass_on(i):
        source = lax.rem(me + N_OWN - lax.rem(STEP * i, N_OWN), N_OWN)
        via, place = in_transit(source, grp, me)

        @pl.when(via)
        def _():
            here = transit.at[at_slot(place)]
            pltpu.make_async_copy(here, here, transit_sem.at[i]).wait()
            pltpu.make_async_remote_copy(
                src_ref=here, dst_ref=land.at[at_slot(i * N_GRP + grp)], send_sem=pass_sem,
                recv_sem=recv_sem.at[i // N_GRP], device_id=(home_row(me), me), device_id_type=MESH,
            ).start()

    def sent(i):
        pltpu.make_async_copy(packed.at[at_slot(0)], packed.at[at_slot(0)], send_sem.at[i]).wait()

    @pl.when(home)
    def _():
        lax.fori_loop(0, N_OWN, lambda i, _: (send(i), 0)[1], 0)

    @pl.when(jnp.logical_not(home))
    def _():
        def step(i, _):
            @pl.when((i >= WINDOW) & (i < N_OWN + WINDOW))
            def _():
                sent(i - WINDOW)

            @pl.when(i < N_OWN)
            def _():
                send(i)

            @pl.when((i >= LAG) & (i < N_OWN + LAG))
            def _():
                pass_on(i - LAG)

            return 0

        lax.fori_loop(0, N_OWN + max(WINDOW, LAG), step, 0)

    def wait(ref, count, sem):
        pltpu.make_async_copy(ref.at[pl.ds(0, count)], ref.at[pl.ds(0, count)], sem).wait()

    cols = iota((128, CHUNK), 1)
    spread = hot(cols - CAP * by_48(cols) == iota((128, CHUNK), 0))
    mine = by_48(iota((CHUNK_MSGS, CHUNK), 1)) == iota((CHUNK_MSGS, CHUNK), 0)

    def pair(a, b, diagonal):
        left = pl.multiple_of(a * CHUNK, CHUNK)
        right = pl.multiple_of(b * CHUNK, CHUNK)
        part = 256
        cols_sum = [jnp.zeros((8, 128), F32)] * (CHUNK // 128)
        for r in range(CHUNK // part):
            rows = pl.ds(left + r * part, part)
            scores = dot_t(unit[rows], unit[pl.ds(right, CHUNK)])
            left_ids = id_col[rows]
            left_scale = scale_col[rows]
            total = row_acc[rows]
            for t in range(CHUNK // 128):
                lanes = pl.ds(right + t * 128, 128)
                scaled = scores[:, t * 128 : (t + 1) * 128] * left_scale * scale_row[0:1, lanes]
                weights = jnp.exp(scaled - SHARPNESS)
                same = left_ids == id_row[0:1, lanes]
                weights = jnp.where(same, weights, 0.0)
                total = total + weights
                if not diagonal:
                    cols_sum[t] = cols_sum[t] + jnp.sum(weights.reshape(part // 8, 8, 128), axis=0)
            row_acc[rows] = total
        if not diagonal:
            for t in range(CHUNK // 128):
                col_acc[:, pl.ds(right + t * 128, 128)] += cols_sum[t]

    @pl.when(home)
    def _():
        sums[...] = jnp.zeros_like(sums)
        row_acc[...] = jnp.zeros_like(row_acc)
        col_acc[...] = jnp.zeros_like(col_acc)
        wait(ids_out, 1, local_sem.at[0])
        sent(0)

        def chunk(a, _):
            @pl.when(a == 0)
            def _():
                wait(ids_in, CHUNK_MSGS - 1, ids_recv_sem.at[0])
                wait(land, CHUNK - CAP, recv_sem.at[0])

            @pl.when(a > 0)
            def _():
                wait(ids_in, CHUNK_MSGS, ids_recv_sem.at[a])
                wait(land, CHUNK, recv_sem.at[a])

            base = pl.multiple_of(a * CHUNK, CHUNK)
            rows = pl.ds(base, CHUNK)
            got = land[rows]
            high = got.astype(BF16)
            unit[rows] = high
            wide = high.astype(F32)
            low = (got - wide).astype(BF16)
            kept = jnp.sum(wide * wide, axis=1, keepdims=True)
            off = jnp.sqrt(jnp.sum(got * got, axis=1, keepdims=True) / jnp.maximum(kept, 1e-30))
            off = jnp.where(kept > 0.0, off - 1.0, 0.0)
            off = jnp.broadcast_to(off, (CHUNK, 128))
            scale_col[rows] = SHARPNESS + SHARPNESS * off
            scale_row[:, rows] = 1.0 + dot_t(hot(iota((8, 128), 1) == 0), off.astype(BF16))
            ids = ids_in[pl.ds(a * CHUNK_MSGS, CHUNK_MSGS), 0, :].astype(BF16)
            in_row = jnp.where(mine, dot(ids, spread), 0.0).astype(BF16)
            row = dot(jnp.ones((8, CHUNK_MSGS), BF16), in_row)
            id_row[:, rows] = row
            at = iota((CHUNK, 128), 0)
            picked = dot(hot(by_48(iota((CHUNK, CHUNK_MSGS), 0)) == iota((CHUNK, CHUNK_MSGS), 1)), ids)
            picked = jnp.where(at - CAP * by_48(at) == iota((CHUNK, 128), 1), picked, 0.0).astype(BF16)
            id_col[rows] = dot(picked, jnp.ones((128, 128), BF16))
            member = hot(iota((CL_OWN, CHUNK), 0).astype(F32) == row[0:1])
            sums[...] += dot(member, high) + dot(member, low)
            lax.fori_loop(0, a, lambda b, _: (pair(a, b, False), 0)[1], 0)
            pair(a, a, True)
            return 0

        lax.fori_loop(0, CHUNKS, chunk, 0)

        def give_back(a, _):
            rows = pl.ds(pl.multiple_of(a * CHUNK, CHUNK), CHUNK)
            part = row_acc[rows]
            high, middle, low = split3(part)
            ones = jnp.ones((8, 128), BF16)
            mass = dot_t(ones, high) + (dot_t(ones, middle) + dot_t(ones, low))
            mass = mass[0:1] + jnp.sum(col_acc[:, rows], axis=0, keepdims=True)
            back = exact(dot_t, jnp.where(mine, mass, 0.0), spread)
            for j in range(CHUNK_MSGS):
                mass_out[a * CHUNK_MSGS + j] = jnp.broadcast_to(back[j : j + 1], (8, 128))
            for j in range(CHUNK_MSGS):
                i = a * (CHUNK_MSGS // N_GRP) + j // N_GRP
                to_grp = j % N_GRP
                to = lax.rem(me + N_OWN - lax.rem(STEP * i, N_OWN), N_OWN)
                here = (to == me) & (grp == to_grp)

                @pl.when(jnp.logical_not(here))
                def _():
                    pltpu.make_async_remote_copy(
                        src_ref=mass_out.at[a * CHUNK_MSGS + j], dst_ref=mass_in.at[me], send_sem=back_send_sem,
                        recv_sem=back_recv_sem, device_id=(to_grp, to), device_id_type=MESH,
                    ).start()

                @pl.when(here)
                def _():
                    pltpu.make_async_copy(mass_out.at[a * CHUNK_MSGS + j], mass_in.at[me], local_sem.at[2]).start()

            return 0

        lax.fori_loop(0, CHUNKS, give_back, 0)

        total = sums[...]
        cen_ref[...] = total * lax.rsqrt(jnp.mean(total * total, axis=1, keepdims=True) + 1e-06)
        for k in range(1, N_GRP):
            pltpu.make_async_remote_copy(
                src_ref=cen_ref, dst_ref=cen_in, send_sem=cen_send_sem.at[k - 1], recv_sem=cen_recv_sem,
                device_id=(lax.rem(grp + k, N_GRP), me), device_id_type=MESH,
            ).start()
        for k in range(1, N_GRP):
            pltpu.make_async_copy(cen_ref, cen_ref, cen_send_sem.at[k - 1]).wait()
        wait(mass_out, MSGS - 1, back_send_sem)
        wait(mass_out, 1, local_sem.at[2])
        wait(mass_in, N_OWN - 1, back_recv_sem)
        lax.fori_loop(1, N_OWN, lambda i, _: (sent(i), 0)[1], 0)
        wait(ids_out, N_OWN - 1, ids_send_sem)

    @pl.when(jnp.logical_not(home))
    def _():
        pltpu.make_async_copy(cen_in, cen_in, cen_recv_sem).wait()
        cen_ref[...] = cen_in[...]
        wait(mass_in, N_OWN, back_recv_sem)

        @pl.when(lax.rem(home_row(me) + grp, 2) == 1)
        def _():
            wait(transit, 16 * CAP, pass_sem)

        wait(ids_out, N_OWN, ids_send_sem)

    got = exact(dot, mass_in[:, 0, :], rank_ref[...])
    mass = jnp.sum(got * rowhot_ref[...], axis=0, keepdims=True)
    score = jnp.broadcast_to(jnp.log(mass), (8, R_DEV))
    target = hot(iota((R_DEV, R_DEV), 0) == order_ref[...])
    dup_ref[...] = exact(dot_t, score, target)[0:1]


def local(embeddings, cluster_ids, owner_map, source_order):
    vmem = pl.BlockSpec(memory_space=pltpu.VMEM)
    dma = pltpu.SemaphoreType.DMA
    dup, centroids = pl.pallas_call(
        kernel,
        out_shape=(jax.ShapeDtypeStruct((1, R_DEV), F32), jax.ShapeDtypeStruct((CL_OWN, D), F32)),
        in_specs=[vmem] * 4,
        out_specs=(vmem, vmem),
        scratch_shapes=[
            pltpu.VMEM((SLOTS, D), F32),
            pltpu.VMEM((N_OWN, 8, 128), F32),
            pltpu.VMEM((MSGS * CAP, D), F32),
            pltpu.VMEM((MSGS, 8, 128), F32),
            pltpu.VMEM((MSGS * CAP, D), BF16),
            pltpu.VMEM((MSGS * CAP, 128), F32),
            pltpu.VMEM((8, MSGS * CAP), F32),
            pltpu.VMEM((MSGS * CAP, 128), F32),
            pltpu.VMEM((8, MSGS * CAP), F32),
            pltpu.VMEM((MSGS * CAP, 128), F32),
            pltpu.VMEM((8, MSGS * CAP), F32),
            pltpu.VMEM((CL_OWN, D), F32),
            pltpu.VMEM((N_OWN, R_DEV), F32),
            pltpu.VMEM((128, R_DEV), BF16),
            pltpu.VMEM((MSGS, 8, 128), F32),
            pltpu.VMEM((N_OWN, 8, 128), F32),
            pltpu.VMEM((CL_OWN, D), F32),
            pltpu.VMEM((16 * CAP, D), F32),
            dma((N_OWN,)), dma((N_OWN,)), dma, dma, dma((CHUNKS,)), dma((CHUNKS,)), dma((3,)), dma, dma, dma((3,)), dma,
        ],
        compiler_params=pltpu.CompilerParams(has_side_effects=True, vmem_limit_bytes=60 << 20),
        name="owner_gather",
    )(
        embeddings,
        cluster_ids.reshape(1, R_DEV),
        owner_map.reshape(1, CLUSTERS),
        source_order.reshape(1, R_DEV),
    )
    return dup.reshape(R_DEV), centroids


def solution(mesh):
    placed = (P(("grp", "own"), None), P(("grp", "own")), P(), P(("grp", "own")))
    return jax.shard_map(
        local,
        mesh=mesh,
        in_specs=placed,
        out_specs=(P(("grp", "own")), P("own", None)),
        check_vma=False,
    )
```

```python
import functools

import jax
import jax.numpy as jnp
from jax import lax
from jax.experimental import pallas as pl
from jax.experimental.pallas import tpu as pltpu
from jax.sharding import PartitionSpec as P

MESH = pl.DeviceIdType.MESH
F32 = jnp.float32
BF16 = jnp.bfloat16

N_GRP = 4
N_OWN = 32
D = 768
R_DEV = 768
CLUSTERS = 512
CL_OWN = 16
CAP = 48
SLOTS = N_OWN * CAP
MSGS = N_GRP * N_OWN
CHUNK_MSGS = 16
CHUNK = CHUNK_MSGS * CAP
CHUNKS = MSGS // CHUNK_MSGS
SHARPNESS = 6.0
SELF = 31
WINDOW = 8
PACKS = 4
LAG = 3


def hot(condition):
    return jnp.where(condition, 1.0, 0.0).astype(BF16)


def iota(shape, dim):
    return lax.broadcasted_iota(jnp.int32, shape, dim)


def by_48(n):
    return (n * 1366) >> 16


def dot(a, b):
    return lax.dot_general(a, b, (((1,), (0,)), ((), ())), preferred_element_type=F32)


def dot_t(a, b):
    return lax.dot_general(a, b, (((1,), (1,)), ((), ())), preferred_element_type=F32)


def split3(a):
    high = a.astype(BF16)
    rest = a - high.astype(F32)
    middle = rest.astype(BF16)
    low = (rest - middle.astype(F32)).astype(BF16)
    return high, middle, low


def exact(product, a, b):
    high, middle, low = split3(a)
    return product(high, b) + (product(middle, b) + product(low, b))


def home_row(owner):
    x, z, core = owner // 8, lax.rem(owner // 2, 4), lax.rem(owner, 2)
    return lax.rem(x + z, 2) + 2 * core


def partner(me, i, back=False):
    a, b, c = lax.rem(i, 4), lax.rem(i // 4, 4), i // 16
    dx = lax.rem(10 - a - b, 4)
    dz = jnp.where(a == 0, 2, jnp.where(a == 1, 1, jnp.where(a == 2, 3, 0)))
    dc = lax.rem(a + c, 2)
    if back:
        dx, dz = 4 - dx, 4 - dz
    x, z, core = me // 8, lax.rem(me // 2, 4), lax.rem(me, 2)
    return lax.rem(x + dx, 4) * 8 + lax.rem(z + dz, 4) * 2 + lax.rem(core + dc, 2)


def step_to(me, owner):
    dx = lax.rem(owner // 8 - me // 8 + 8, 4)
    dz = lax.rem(lax.rem(owner // 2, 4) - lax.rem(me // 2, 4) + 4, 4)
    dc = lax.rem(owner + me, 2)
    a = jnp.where(dz == 2, 0, jnp.where(dz == 1, 1, jnp.where(dz == 3, 2, 3)))
    return a + 4 * lax.rem(18 - a - dx, 4) + 16 * lax.rem(dc + a, 2)


def in_transit(source, grp, owner):
    z_step = lax.rem(owner // 2 - source // 2 + 2 * N_OWN, 4)
    y_step = lax.rem(home_row(owner) - grp + 4, 4)
    via = ((y_step == 1) & (z_step >= 2)) | ((y_step == 3) & (z_step >= 1) & (z_step <= 2))
    late = jnp.where(y_step == 1, z_step - 2, z_step - 1)
    return via, late * 8 + source // 8 * 2 + lax.rem(source, 2)


def kernel(
    x_ref, cid_ref, map_ref, order_ref, dup_ref, cen_ref,
    packed, ids_out, land, ids_in, unit, row_acc, col_acc, id_col, id_row, scale_col, scale_row, sums, rowhot_ref, rank_ref,
    mass_out, mass_in, cen_in, transit, x_held,
    send_sem, transit_sem, pass_sem, ids_send_sem, recv_sem, ids_recv_sem, local_sem, back_send_sem, back_recv_sem, cen_send_sem, cen_recv_sem,
):
    me, grp = lax.axis_index("own"), lax.axis_index("grp")
    home = grp == home_row(me)

    barrier = pltpu.get_barrier_semaphore()

    def tell(grp_to, own_to):
        pl.semaphore_signal(barrier, inc=1, device_id=(grp_to, own_to), device_id_type=MESH)

    def tell_home(o, _):
        to = home_row(o)

        @pl.when(jnp.logical_not(home & (o == me)))
        def _():
            tell(to, o)

        return 0

    lax.fori_loop(0, N_OWN, tell_home, 0)

    @pl.when(home)
    def _():
        def tell_others(m, _):
            @pl.when(home_row(m // N_GRP) != lax.rem(m, N_GRP))
            def _():
                tell(lax.rem(m, N_GRP), m // N_GRP)

            return 0

        lax.fori_loop(0, MSGS, tell_others, 0)

    @pl.when(jnp.logical_not(home))
    def _():
        def tell_senders(o, _):
            @pl.when(in_transit(o, grp, me)[0] & (home_row(o) != grp))
            def _():
                tell(grp, o)

            return 0

        lax.fori_loop(0, N_OWN, tell_senders, 0)

    x_copy = pltpu.make_async_copy(x_ref, x_held, local_sem.at[1])
    x_copy.start()

    owner_hot = hot(iota((N_OWN, CLUSTERS), 0) == map_ref[...].reshape(1, CLUSTERS))
    earlier = hot(iota((CLUSTERS, CLUSTERS), 0) < iota((CLUSTERS, CLUSTERS), 1))
    before = dot(owner_hot, earlier)
    place = jnp.sum(owner_hot.astype(F32) * before, axis=0, keepdims=True)
    table = jnp.concatenate([owner_hot, jnp.broadcast_to(place, (16, CLUSTERS)).astype(BF16)], axis=0)
    looked_up = dot(table, hot(iota((CLUSTERS, R_DEV), 0) == cid_ref[...].reshape(1, R_DEV)))
    row_hot, row_place = looked_up[:N_OWN], looked_up[N_OWN : N_OWN + 1]
    ahead = hot(iota((R_DEV, R_DEV), 0) < iota((R_DEV, R_DEV), 1))
    rank = jnp.sum(row_hot * dot(row_hot.astype(BF16), ahead), axis=0, keepdims=True)
    owner = jnp.sum(row_hot * iota((N_OWN, R_DEV), 0).astype(F32), axis=0, keepdims=True)
    rank = rank.astype(jnp.int32)
    slot = step_to(me, owner.astype(jnp.int32)) * CAP + rank
    rank_hot = hot(iota((128, R_DEV), 0) == rank)
    rowhot_ref[...] = row_hot
    rank_ref[...] = rank_hot
    ids = dot_t((row_hot * (row_place + 1.0)).astype(BF16), rank_hot) - 1.0
    ids_out[:, 0, :] = ids

    x_copy.wait()
    x = x_held[...]
    u = x * lax.rsqrt(jnp.sum(x * x, axis=1, keepdims=True) + 1e-06)
    high = u.astype(BF16)
    low = (u - high.astype(F32)).astype(BF16)
    block = SLOTS // PACKS

    def pack(k):
        pick = hot(iota((block, R_DEV), 0) + k * block == slot)
        packed[pl.ds(k * block, block)] = dot(pick, high) + dot(pick, low)

    pack(0)

    @pl.when(home)
    def _():
        pl.semaphore_wait(barrier, MSGS - 1)

    @pl.when(jnp.logical_not(home))
    def _():
        pl.semaphore_wait(barrier, N_OWN + 8)

    def at_slot(m):
        return pl.ds(pl.multiple_of(m * CAP, CAP), CAP)

    def send(i):
        o = partner(me, i)
        to = home_row(o)
        here = (o == me) & (to == grp)
        via, place = in_transit(me, grp, o)
        m = i * N_GRP + grp

        @pl.when(jnp.logical_not(here))
        def _():
            pltpu.make_async_remote_copy(
                src_ref=ids_out.at[o], dst_ref=ids_in.at[m], send_sem=ids_send_sem,
                recv_sem=ids_recv_sem.at[i // N_GRP], device_id=(to, o), device_id_type=MESH,
            ).start()

        @pl.when(jnp.logical_not(here | via))
        def _():
            pltpu.make_async_remote_copy(
                src_ref=packed.at[at_slot(i)], dst_ref=land.at[at_slot(m)], send_sem=send_sem.at[i],
                recv_sem=recv_sem.at[i // N_GRP], device_id=(to, o), device_id_type=MESH,
            ).start()

        @pl.when(via)
        def _():
            pltpu.make_async_remote_copy(
                src_ref=packed.at[at_slot(i)], dst_ref=transit.at[at_slot(place)], send_sem=send_sem.at[i],
                recv_sem=transit_sem.at[i], device_id=(grp, o), device_id_type=MESH,
            ).start()

        @pl.when(here)
        def _():
            pltpu.make_async_copy(ids_out.at[o], ids_in.at[m], local_sem.at[0]).start()
            pltpu.make_async_copy(packed.at[at_slot(i)], land.at[at_slot(m)], send_sem.at[i]).start()

    def pass_on(i):
        source = partner(me, i, back=True)
        via, place = in_transit(source, grp, me)

        @pl.when(via)
        def _():
            here = transit.at[at_slot(place)]
            pltpu.make_async_copy(here, here, transit_sem.at[i]).wait()
            pltpu.make_async_remote_copy(
                src_ref=here, dst_ref=land.at[at_slot(i * N_GRP + grp)], send_sem=pass_sem,
                recv_sem=recv_sem.at[i // N_GRP], device_id=(home_row(me), me), device_id_type=MESH,
            ).start()

    def sent(i):
        pltpu.make_async_copy(packed.at[at_slot(0)], packed.at[at_slot(0)], send_sem.at[i]).wait()

    def step(i, _):
        @pl.when(jnp.logical_not(home) & (i >= WINDOW) & (i < N_OWN + WINDOW))
        def _():
            sent(i - WINDOW)

        @pl.when(i < N_OWN)
        def _():
            send(i)

        @pl.when((i >= LAG) & (i < N_OWN + LAG))
        def _():
            pass_on(i - LAG)

        return 0

    for k in range(PACKS):
        if k:
            pack(k)
        group = N_OWN // PACKS
        lax.fori_loop(k * group, (k + 1) * group, step, 0)
    lax.fori_loop(N_OWN, N_OWN + max(WINDOW, LAG), step, 0)

    def wait(ref, count, sem):
        pltpu.make_async_copy(ref.at[pl.ds(0, count)], ref.at[pl.ds(0, count)], sem).wait()

    cols = iota((128, CHUNK), 1)
    spread = hot(cols - CAP * by_48(cols) == iota((128, CHUNK), 0))
    mine = by_48(iota((CHUNK_MSGS, CHUNK), 1)) == iota((CHUNK_MSGS, CHUNK), 0)

    def pair(a, b, diagonal):
        left = pl.multiple_of(a * CHUNK, CHUNK)
        right = pl.multiple_of(b * CHUNK, CHUNK)
        part = 256
        cols_sum = [jnp.zeros((8, 128), F32)] * (CHUNK // 128)
        for r in range(CHUNK // part):
            rows = pl.ds(left + r * part, part)
            scores = dot_t(unit[rows], unit[pl.ds(right, CHUNK)])
            left_ids = id_col[rows]
            left_scale = scale_col[rows]
            total = row_acc[rows]
            for t in range(CHUNK // 128):
                lanes = pl.ds(right + t * 128, 128)
                scaled = scores[:, t * 128 : (t + 1) * 128] * left_scale * scale_row[0:1, lanes]
                weights = jnp.exp(scaled)
                same = left_ids == id_row[0:1, lanes]
                weights = jnp.where(same, weights, 0.0)
                total = total + weights
                if not diagonal:
                    cols_sum[t] = cols_sum[t] + jnp.sum(weights.reshape(part // 8, 8, 128), axis=0)
            row_acc[rows] = total
        if not diagonal:
            for t in range(CHUNK // 128):
                col_acc[:, pl.ds(right + t * 128, 128)] += cols_sum[t]

    @pl.when(home)
    def _():
        sums[...] = jnp.zeros_like(sums)
        row_acc[...] = jnp.zeros_like(row_acc)
        col_acc[...] = jnp.zeros_like(col_acc)
        wait(ids_out, 1, local_sem.at[0])
        sent(SELF)

        def prepare(a):
            @pl.when(a == SELF // N_GRP)
            def _():
                wait(ids_in, CHUNK_MSGS - 1, ids_recv_sem.at[SELF // N_GRP])
                wait(land, CHUNK - CAP, recv_sem.at[SELF // N_GRP])

            @pl.when(a != SELF // N_GRP)
            def _():
                wait(ids_in, CHUNK_MSGS, ids_recv_sem.at[a])
                wait(land, CHUNK, recv_sem.at[a])

            base = pl.multiple_of(a * CHUNK, CHUNK)
            rows = pl.ds(base, CHUNK)
            got = land[rows]
            high = got.astype(BF16)
            unit[rows] = high
            wide = high.astype(F32)
            low = (got - wide).astype(BF16)
            kept = jnp.sum(wide * wide, axis=1, keepdims=True)
            off = jnp.sqrt(jnp.sum(got * got, axis=1, keepdims=True) / jnp.maximum(kept, 1e-30))
            off = jnp.where(kept > 0.0, off - 1.0, 0.0)
            off = jnp.broadcast_to(off, (CHUNK, 128))
            scale_col[rows] = SHARPNESS + SHARPNESS * off
            scale_row[:, rows] = 1.0 + dot_t(hot(iota((8, 128), 1) == 0), off.astype(BF16))
            ids = ids_in[pl.ds(a * CHUNK_MSGS, CHUNK_MSGS), 0, :].astype(BF16)
            in_row = jnp.where(mine, dot(ids, spread), 0.0).astype(BF16)
            row = dot(jnp.ones((8, CHUNK_MSGS), BF16), in_row)
            id_row[:, rows] = row
            at = iota((CHUNK, 128), 0)
            picked = dot(hot(by_48(iota((CHUNK, CHUNK_MSGS), 0)) == iota((CHUNK, CHUNK_MSGS), 1)), ids)
            picked = jnp.where(at - CAP * by_48(at) == iota((CHUNK, 128), 1), picked, 0.0).astype(BF16)
            id_col[rows] = dot(picked, jnp.ones((128, 128), BF16))
            member = hot(iota((CL_OWN, CHUNK), 0).astype(F32) == row[0:1])
            sums[...] += dot(member, high) + dot(member, low)

        def chunk(a, _):
            prepare(a)
            lax.fori_loop(0, a, lambda b, _: (pair(a, b, False), 0)[1], 0)
            pair(a, a, True)
            return 0

        last = CHUNKS - 1
        lax.fori_loop(0, last, chunk, 0)
        prepare(last)
        total = sums[...]
        cen_ref[...] = total * lax.rsqrt(jnp.mean(total * total, axis=1, keepdims=True) + 1e-06)
        for k in range(1, N_GRP):
            pltpu.make_async_remote_copy(
                src_ref=cen_ref, dst_ref=cen_in, send_sem=cen_send_sem.at[k - 1], recv_sem=cen_recv_sem,
                device_id=(lax.rem(grp + k, N_GRP), me), device_id_type=MESH,
            ).start()

        def give_back(a):
            rows = pl.ds(pl.multiple_of(a * CHUNK, CHUNK), CHUNK)
            part = row_acc[rows]
            high, middle, low = split3(part)
            ones = jnp.ones((8, 128), BF16)
            mass = dot_t(ones, high) + (dot_t(ones, middle) + dot_t(ones, low))
            mass = mass[0:1] + jnp.sum(col_acc[:, rows], axis=0, keepdims=True)
            back = exact(dot_t, jnp.where(mine, mass, 0.0), spread)
            mass_out[pl.ds(a * CHUNK_MSGS, CHUNK_MSGS), 0, :] = back
            for j in range(CHUNK_MSGS):
                i = a * (CHUNK_MSGS // N_GRP) + j // N_GRP
                to_grp = j % N_GRP
                to = partner(me, i, back=True)
                here = (to == me) & (grp == to_grp)

                @pl.when(jnp.logical_not(here))
                def _():
                    pltpu.make_async_remote_copy(
                        src_ref=mass_out.at[a * CHUNK_MSGS + j], dst_ref=mass_in.at[me], send_sem=back_send_sem,
                        recv_sem=back_recv_sem, device_id=(to_grp, to), device_id_type=MESH,
                    ).start()

                @pl.when(here)
                def _():
                    pltpu.make_async_copy(mass_out.at[a * CHUNK_MSGS + j], mass_in.at[me], local_sem.at[2]).start()

        def finish(b, _):
            pair(last, b, False)
            give_back(b)
            return 0

        lax.fori_loop(0, last, finish, 0)
        pair(last, last, True)
        give_back(last)

        for k in range(1, N_GRP):
            pltpu.make_async_copy(cen_ref, cen_ref, cen_send_sem.at[k - 1]).wait()
        wait(mass_out, MSGS - 1, back_send_sem)
        wait(mass_out, 1, local_sem.at[2])
        wait(mass_in, N_OWN - 1, back_recv_sem)
        lax.fori_loop(0, N_OWN - 1, lambda i, _: (sent(lax.rem(SELF + 1 + i, N_OWN)), 0)[1], 0)
        wait(ids_out, N_OWN - 1, ids_send_sem)

    @pl.when(jnp.logical_not(home))
    def _():
        pltpu.make_async_copy(cen_in, cen_in, cen_recv_sem).wait()
        cen_ref[...] = cen_in[...]
        wait(mass_in, N_OWN, back_recv_sem)

        @pl.when(lax.rem(home_row(me) + grp, 2) == 1)
        def _():
            wait(transit, 16 * CAP, pass_sem)

        wait(ids_out, N_OWN, ids_send_sem)

    got = exact(dot, mass_in[:, 0, :], rank_ref[...])
    mass = jnp.sum(got * rowhot_ref[...], axis=0, keepdims=True)
    score = jnp.broadcast_to(jnp.log(mass) - SHARPNESS, (8, R_DEV))
    target = hot(iota((R_DEV, R_DEV), 0) == order_ref[...].reshape(1, R_DEV))
    dup_ref[...] = exact(dot_t, score, target)[0:1].reshape(R_DEV)


def local(embeddings, cluster_ids, owner_map, source_order):
    vmem = pl.BlockSpec(memory_space=pltpu.VMEM)
    dma = pltpu.SemaphoreType.DMA
    dup, centroids = pl.pallas_call(
        kernel,
        out_shape=(jax.ShapeDtypeStruct((R_DEV,), F32), jax.ShapeDtypeStruct((CL_OWN, D), F32)),
        in_specs=[pl.BlockSpec(memory_space=pl.ANY)] + [vmem] * 3,
        out_specs=(vmem, vmem),
        scratch_shapes=[
            pltpu.VMEM((SLOTS, D), F32),
            pltpu.VMEM((N_OWN, 1, 128), F32),
            pltpu.VMEM((MSGS * CAP, D), F32),
            pltpu.VMEM((MSGS, 1, 128), F32),
            pltpu.VMEM((MSGS * CAP, D), BF16),
            pltpu.VMEM((MSGS * CAP, 128), F32),
            pltpu.VMEM((8, MSGS * CAP), F32),
            pltpu.VMEM((MSGS * CAP, 128), F32),
            pltpu.VMEM((8, MSGS * CAP), F32),
            pltpu.VMEM((MSGS * CAP, 128), F32),
            pltpu.VMEM((8, MSGS * CAP), F32),
            pltpu.VMEM((CL_OWN, D), F32),
            pltpu.VMEM((N_OWN, R_DEV), F32),
            pltpu.VMEM((128, R_DEV), BF16),
            pltpu.VMEM((MSGS, 1, 128), F32),
            pltpu.VMEM((N_OWN, 1, 128), F32),
            pltpu.VMEM((CL_OWN, D), F32),
            pltpu.VMEM((16 * CAP, D), F32),
            pltpu.VMEM((R_DEV, D), F32),
            dma((N_OWN,)), dma((N_OWN,)), dma, dma, dma((CHUNKS,)), dma((CHUNKS,)), dma((3,)), dma, dma, dma((3,)), dma,
        ],
        compiler_params=pltpu.CompilerParams(collective_id=0, has_side_effects=True, vmem_limit_bytes=60 << 20),
        name="owner_gather",
    )(
        embeddings,
        cluster_ids,
        owner_map,
        source_order,
    )
    return dup, centroids


def solution(mesh):
    placed = (P(("grp", "own"), None), P(("grp", "own")), P(), P(("grp", "own")))
    return jax.shard_map(
        local,
        mesh=mesh,
        in_specs=placed,
        out_specs=(P(("grp", "own")), P("own", None)),
        check_vma=False,
    )
```

```python
import functools

import jax
import jax.numpy as jnp
from jax import lax
from jax.experimental import pallas as pl
from jax.experimental.pallas import tpu as pltpu
from jax.sharding import PartitionSpec as P

MESH = pl.DeviceIdType.MESH
F32 = jnp.float32
BF16 = jnp.bfloat16

N_GRP = 4
N_OWN = 32
D = 768
R_DEV = 768
CLUSTERS = 512
CL_OWN = 16
CAP = 48
SLOTS = N_OWN * CAP
MSGS = N_GRP * N_OWN
CHUNK_MSGS = 16
CHUNK = CHUNK_MSGS * CAP
CHUNKS = MSGS // CHUNK_MSGS
SHARPNESS = 6.0
RELAYED = (4, 7)
SELF = 31
SELF_CHUNK = 6
WINDOW = 12
PACKS = 4
PART = 256
LAG = 5


def hot(condition):
    return jnp.where(condition, 1.0, 0.0).astype(BF16)


def iota(shape, dim):
    return lax.broadcasted_iota(jnp.int32, shape, dim)


def by_48(n):
    return (n * 1366) >> 16


def dot(a, b):
    return lax.dot_general(a, b, (((1,), (0,)), ((), ())), preferred_element_type=F32)


def dot_t(a, b):
    return lax.dot_general(a, b, (((1,), (1,)), ((), ())), preferred_element_type=F32)


def split3(a):
    high = a.astype(BF16)
    rest = a - high.astype(F32)
    middle = rest.astype(BF16)
    low = (rest - middle.astype(F32)).astype(BF16)
    return high, middle, low


def exact(product, a, b):
    rows = a.shape[0]
    out = product(jnp.concatenate(split3(a), axis=0), b)
    return out[:rows] + (out[rows : 2 * rows] + out[2 * rows :])


def home_row(owner):
    x, z, core = owner // 8, lax.rem(owner // 2, 4), lax.rem(owner, 2)
    return lax.rem(x + z, 2) + 2 * core


def partner(me, i, back=False):
    a, b, c = lax.rem(i, 4), lax.rem(i // 4, 4), i // 16
    dx = lax.rem(10 - a - b, 4)
    dz = jnp.where(a == 0, 2, jnp.where(a == 1, 1, jnp.where(a == 2, 3, 0)))
    dc = lax.rem(a + c, 2)
    if back:
        dx, dz = 4 - dx, 4 - dz
    x, z, core = me // 8, lax.rem(me // 2, 4), lax.rem(me, 2)
    return lax.rem(x + dx, 4) * 8 + lax.rem(z + dz, 4) * 2 + lax.rem(core + dc, 2)


def step_to(me, owner):
    dx = lax.rem(owner // 8 - me // 8 + 8, 4)
    dz = lax.rem(lax.rem(owner // 2, 4) - lax.rem(me // 2, 4) + 4, 4)
    dc = lax.rem(owner + me, 2)
    a = jnp.where(dz == 2, 0, jnp.where(dz == 1, 1, jnp.where(dz == 3, 2, 3)))
    return a + 4 * lax.rem(18 - a - dx, 4) + 16 * lax.rem(dc + a, 2)


def in_transit(source, grp, owner):
    z_step = lax.rem(owner // 2 - source // 2 + 2 * N_OWN, 4)
    y_step = lax.rem(home_row(owner) - grp + 4, 4)
    via = ((y_step == 1) & (z_step >= 2)) | ((y_step == 3) & (z_step >= 1) & (z_step <= 2))
    late = jnp.where(y_step == 1, z_step - 2, z_step - 1)
    return via, late * 8 + source // 8 * 2 + lax.rem(source, 2)


def place_of(i, y_step):
    group, a = i // 4, lax.rem(i, 4)
    via = ((a == 0) & (lax.rem(y_step, 2) == 1)) | ((a == 1) & (y_step == 3)) | ((a == 2) & (y_step == 1))
    early = jnp.where(
        a == 0, y_step // 2, jnp.where(a == 1, 2 + y_step, jnp.where(a == 2, 5 + jnp.maximum(y_step - 1, 0), 8 + y_step))
    )
    n = jnp.where(via, 4 * group + jnp.where(a == 0, y_step // 2, a + 1), 12 * group + early)
    k = n // CHUNK_MSGS
    late = jnp.where(k == 0, RELAYED[0], RELAYED[1])
    k = jnp.where(via, late, k + jnp.where(k >= RELAYED[0], 1, 0))
    return k * CHUNK_MSGS + lax.rem(n, CHUNK_MSGS)


def messages():
    early, late = [], []
    for i in range(N_OWN):
        for y_step in range(N_GRP):
            via = (i % 4, y_step) in ((0, 1), (0, 3), (1, 3), (2, 1))
            (late if via else early).append((i, y_step))
    first = RELAYED[0] * CHUNK_MSGS
    return early[:first] + late[:CHUNK_MSGS] + early[first:] + late[CHUNK_MSGS:]


def kernel(
    x_ref, cid_ref, map_ref, order_ref, dup_ref, cen_ref,
    packed, ids_out, land, ids_in, unit, row_acc, col_acc, id_col, id_row, scale_col, scale_row, sums, rowhot_ref, rank_ref,
    mass_out, mass_in, cen_in, transit, x_held, target_ref,
    send_sem, transit_sem, pass_sem, ids_send_sem, recv_sem, ids_recv_sem, local_sem, back_send_sem, back_recv_sem, cen_send_sem, cen_recv_sem,
):
    me, grp = lax.axis_index("own"), lax.axis_index("grp")
    home = grp == home_row(me)

    barrier = pltpu.get_barrier_semaphore()

    def tell(grp_to, own_to):
        pl.semaphore_signal(barrier, inc=1, device_id=(grp_to, own_to), device_id_type=MESH)

    def tell_home(o, _):
        to = home_row(o)

        @pl.when(jnp.logical_not(home & (o == me)))
        def _():
            tell(to, o)

        return 0

    lax.fori_loop(0, N_OWN, tell_home, 0)

    @pl.when(home)
    def _():
        def tell_others(m, _):
            @pl.when(home_row(m // N_GRP) != lax.rem(m, N_GRP))
            def _():
                tell(lax.rem(m, N_GRP), m // N_GRP)

            return 0

        lax.fori_loop(0, MSGS, tell_others, 0)

    @pl.when(jnp.logical_not(home))
    def _():
        def tell_senders(o, _):
            @pl.when(in_transit(o, grp, me)[0] & (home_row(o) != grp))
            def _():
                tell(grp, o)

            return 0

        lax.fori_loop(0, N_OWN, tell_senders, 0)

    x_copy = pltpu.make_async_copy(x_ref, x_held, local_sem.at[1])
    x_copy.start()

    owner_hot = hot(iota((N_OWN, CLUSTERS), 0) == map_ref[...].reshape(1, CLUSTERS))
    earlier = hot(iota((CLUSTERS, CLUSTERS), 0) < iota((CLUSTERS, CLUSTERS), 1))
    before = dot(owner_hot, earlier)
    place = jnp.sum(owner_hot.astype(F32) * before, axis=0, keepdims=True)
    table = jnp.concatenate([owner_hot, jnp.broadcast_to(place, (16, CLUSTERS)).astype(BF16)], axis=0)
    looked_up = dot(table, hot(iota((CLUSTERS, R_DEV), 0) == cid_ref[...].reshape(1, R_DEV)))
    row_hot, row_place = looked_up[:N_OWN], looked_up[N_OWN : N_OWN + 1]
    ahead = hot(iota((R_DEV, R_DEV), 0) < iota((R_DEV, R_DEV), 1))
    rank = jnp.sum(row_hot * dot(row_hot.astype(BF16), ahead), axis=0, keepdims=True)
    owner = jnp.sum(row_hot * iota((N_OWN, R_DEV), 0).astype(F32), axis=0, keepdims=True)
    rank = rank.astype(jnp.int32)
    slot = step_to(me, owner.astype(jnp.int32)) * CAP + rank
    rank_hot = hot(iota((128, R_DEV), 0) == rank)
    rowhot_ref[...] = row_hot
    rank_ref[...] = rank_hot
    ids = dot_t((row_hot * (row_place + 1.0)).astype(BF16), rank_hot) - 1.0
    ids_out[:, 0, :] = ids

    x_copy.wait()
    x = x_held[...]
    u = x * lax.rsqrt(jnp.sum(x * x, axis=1, keepdims=True) + 1e-06)
    high = u.astype(BF16)
    low = (u - high.astype(F32)).astype(BF16)
    block = SLOTS // PACKS

    def pack(k):
        pick = hot(iota((block, R_DEV), 0) + k * block == slot)
        packed[pl.ds(k * block, block)] = dot(pick, high) + dot(pick, low)

    pack(0)

    @pl.when(home)
    def _():
        pl.semaphore_wait(barrier, MSGS - 1)

    @pl.when(jnp.logical_not(home))
    def _():
        pl.semaphore_wait(barrier, N_OWN + 8)

    def at_slot(m):
        return pl.ds(pl.multiple_of(m * CAP, CAP), CAP)

    def send(i):
        o = partner(me, i)
        to = home_row(o)
        here = (o == me) & (to == grp)
        via, place = in_transit(me, grp, o)
        m = place_of(i, lax.rem(to - grp + N_GRP, N_GRP))
        part = m // CHUNK_MSGS

        @pl.when(jnp.logical_not(here))
        def _():
            pltpu.make_async_remote_copy(
                src_ref=ids_out.at[o], dst_ref=ids_in.at[m], send_sem=ids_send_sem,
                recv_sem=ids_recv_sem.at[part], device_id=(to, o), device_id_type=MESH,
            ).start()

        @pl.when(jnp.logical_not(here | via))
        def _():
            pltpu.make_async_remote_copy(
                src_ref=packed.at[at_slot(i)], dst_ref=land.at[at_slot(m)], send_sem=send_sem.at[i],
                recv_sem=recv_sem.at[part], device_id=(to, o), device_id_type=MESH,
            ).start()

        @pl.when(via)
        def _():
            pltpu.make_async_remote_copy(
                src_ref=packed.at[at_slot(i)], dst_ref=transit.at[at_slot(place)], send_sem=send_sem.at[i],
                recv_sem=transit_sem.at[i], device_id=(grp, o), device_id_type=MESH,
            ).start()

        @pl.when(here)
        def _():
            pltpu.make_async_copy(ids_out.at[o], ids_in.at[m], local_sem.at[0]).start()
            pltpu.make_async_copy(packed.at[at_slot(i)], land.at[at_slot(m)], send_sem.at[i]).start()

    def pass_on(i):
        source = partner(me, i, back=True)
        via, place = in_transit(source, grp, me)

        @pl.when(via)
        def _():
            m = place_of(i, lax.rem(home_row(me) - grp + N_GRP, N_GRP))
            here = transit.at[at_slot(place)]
            pltpu.make_async_copy(here, here, transit_sem.at[i]).wait()
            pltpu.make_async_remote_copy(
                src_ref=here, dst_ref=land.at[at_slot(m)], send_sem=pass_sem,
                recv_sem=recv_sem.at[m // CHUNK_MSGS], device_id=(home_row(me), me), device_id_type=MESH,
            ).start()

    def sent(i):
        pltpu.make_async_copy(packed.at[at_slot(0)], packed.at[at_slot(0)], send_sem.at[i]).wait()

    def step(i, _):
        @pl.when(jnp.logical_not(home) & (i >= WINDOW) & (i < N_OWN + WINDOW))
        def _():
            sent(i - WINDOW)

        @pl.when(i < N_OWN)
        def _():
            send(i)

        @pl.when((i >= LAG) & (i < N_OWN + LAG))
        def _():
            pass_on(i - LAG)

        return 0

    for k in range(PACKS):
        if k:
            pack(k)
        group = N_OWN // PACKS
        lax.fori_loop(k * group, (k + 1) * group, step, 0)
    lax.fori_loop(N_OWN, N_OWN + max(WINDOW, LAG), step, 0)

    def wait(ref, count, sem):
        pltpu.make_async_copy(ref.at[pl.ds(0, count)], ref.at[pl.ds(0, count)], sem).wait()

    target_ref[...] = hot(iota((R_DEV, R_DEV), 0) == order_ref[...].reshape(1, R_DEV))
    cols = iota((128, CHUNK), 1)
    spread = hot(cols - CAP * by_48(cols) == iota((128, CHUNK), 0))
    mine = by_48(iota((CHUNK_MSGS, CHUNK), 1)) == iota((CHUNK_MSGS, CHUNK), 0)

    def weigh(rows, right, width, only_rows):
        scores = dot_t(unit[rows], unit[pl.ds(right, width)])
        left_ids, left_scale, total = id_col[rows], scale_col[rows], row_acc[rows]
        columns = []
        for t in range(width // 128):
            lanes = pl.ds(right + t * 128, 128)
            weights = jnp.exp(scores[:, t * 128 : (t + 1) * 128] * left_scale * scale_row[0:1, lanes])
            weights = jnp.where(left_ids == id_row[0:1, lanes], weights, 0.0)
            total = total + weights
            if t < only_rows:
                columns.append(jnp.sum(weights.reshape(PART // 8, 8, 128), axis=0))
        row_acc[rows] = total
        return columns

    def add_columns(right, columns):
        for t, column in enumerate(columns):
            col_acc[:, pl.ds(right + t * 128, 128)] += column

    def pair(a, b):
        left = pl.multiple_of(a * CHUNK, CHUNK)
        right = pl.multiple_of(b * CHUNK, CHUNK)
        parts = [weigh(pl.ds(left + r * PART, PART), right, CHUNK, CHUNK // 128) for r in range(CHUNK // PART)]
        add_columns(right, [sum(each) for each in zip(*parts)])

    def inner(a):
        left = pl.multiple_of(a * CHUNK, CHUNK)
        for r in range(CHUNK // PART):
            add_columns(left, weigh(pl.ds(left + r * PART, PART), left, (r + 1) * PART, r * PART // 128))

    @pl.when(home)
    def _():
        sums[...] = jnp.zeros_like(sums)
        row_acc[...] = jnp.zeros_like(row_acc)
        col_acc[...] = jnp.zeros_like(col_acc)
        wait(ids_out, 1, local_sem.at[0])
        sent(SELF)

        def prepare(a):
            @pl.when(a == SELF_CHUNK)
            def _():
                wait(ids_in, CHUNK_MSGS - 1, ids_recv_sem.at[SELF_CHUNK])
                wait(land, CHUNK - CAP, recv_sem.at[SELF_CHUNK])

            @pl.when(a != SELF_CHUNK)
            def _():
                wait(ids_in, CHUNK_MSGS, ids_recv_sem.at[a])
                wait(land, CHUNK, recv_sem.at[a])

            base = pl.multiple_of(a * CHUNK, CHUNK)
            rows = pl.ds(base, CHUNK)
            got = land[rows]
            high = got.astype(BF16)
            unit[rows] = high
            wide = high.astype(F32)
            low = (got - wide).astype(BF16)
            kept = jnp.sum(wide * wide, axis=1, keepdims=True)
            off = jnp.sqrt(jnp.sum(got * got, axis=1, keepdims=True) / jnp.maximum(kept, 1e-30))
            off = jnp.where(kept > 0.0, off - 1.0, 0.0)
            off = jnp.broadcast_to(off, (CHUNK, 128))
            scale_col[rows] = SHARPNESS + SHARPNESS * off
            scale_row[:, rows] = 1.0 + dot_t(hot(iota((8, 128), 1) == 0), off.astype(BF16))
            ids = ids_in[pl.ds(a * CHUNK_MSGS, CHUNK_MSGS), 0, :].astype(BF16)
            in_row = jnp.where(mine, dot(ids, spread), 0.0).astype(BF16)
            row = dot(jnp.ones((8, CHUNK_MSGS), BF16), in_row)
            id_row[:, rows] = row
            at = iota((CHUNK, 128), 0)
            picked = dot(hot(by_48(iota((CHUNK, CHUNK_MSGS), 0)) == iota((CHUNK, CHUNK_MSGS), 1)), ids)
            picked = jnp.where(at - CAP * by_48(at) == iota((CHUNK, 128), 1), picked, 0.0).astype(BF16)
            id_col[rows] = dot(picked, jnp.ones((128, 128), BF16))
            member = hot(iota((CL_OWN, CHUNK), 0).astype(F32) == row[0:1])
            sums[...] += dot(member, high) + dot(member, low)

        def chunk(a, _):
            prepare(a)
            lax.fori_loop(0, a, lambda b, _: (pair(a, b), 0)[1], 0)
            inner(a)
            return 0

        last = CHUNKS - 1
        lax.fori_loop(0, last, chunk, 0)
        prepare(last)
        total = sums[...]
        cen_ref[...] = total * lax.rsqrt(jnp.mean(total * total, axis=1, keepdims=True) + 1e-06)
        for k in range(1, N_GRP):
            pltpu.make_async_remote_copy(
                src_ref=cen_ref, dst_ref=cen_in, send_sem=cen_send_sem.at[k - 1], recv_sem=cen_recv_sem,
                device_id=(lax.rem(grp + k, N_GRP), me), device_id_type=MESH,
            ).start()

        order = messages()

        def give_back(a):
            rows = pl.ds(a * CHUNK, CHUNK)
            part = row_acc[rows]
            high, middle, low = split3(part)
            ones = jnp.ones((8, 128), BF16)
            mass = dot_t(ones, high) + (dot_t(ones, middle) + dot_t(ones, low))
            mass = mass[0:1] + jnp.sum(col_acc[:, rows], axis=0, keepdims=True)
            back = exact(dot_t, jnp.where(mine, mass, 0.0), spread)
            mass_out[pl.ds(a * CHUNK_MSGS, CHUNK_MSGS), 0, :] = back
            for j in range(CHUNK_MSGS):
                i, y_step = order[a * CHUNK_MSGS + j]
                to_grp = lax.rem(grp + N_GRP - y_step, N_GRP)
                to = partner(me, i, back=True)
                here = (i, y_step) == (SELF, 0)

                block = mass_out.at[a * CHUNK_MSGS + j]
                if here:
                    pltpu.make_async_copy(block, mass_in.at[me], local_sem.at[2]).start()
                else:
                    pltpu.make_async_remote_copy(
                        src_ref=block, dst_ref=mass_in.at[me], send_sem=back_send_sem,
                        recv_sem=back_recv_sem, device_id=(to_grp, to), device_id_type=MESH,
                    ).start()

        lax.fori_loop(0, last, lambda b, _: (pair(last, b), 0)[1], 0)
        inner(last)
        for a in range(CHUNKS):
            give_back(a)

        for k in range(1, N_GRP):
            pltpu.make_async_copy(cen_ref, cen_ref, cen_send_sem.at[k - 1]).wait()
        wait(mass_out, MSGS - 1, back_send_sem)
        wait(mass_out, 1, local_sem.at[2])
        wait(mass_in, N_OWN - 1, back_recv_sem)
        lax.fori_loop(0, N_OWN - 1, lambda i, _: (sent(lax.rem(SELF + 1 + i, N_OWN)), 0)[1], 0)
        wait(ids_out, N_OWN - 1, ids_send_sem)

    @pl.when(jnp.logical_not(home))
    def _():
        pltpu.make_async_copy(cen_in, cen_in, cen_recv_sem).wait()
        cen_ref[...] = cen_in[...]
        wait(mass_in, N_OWN, back_recv_sem)

        @pl.when(lax.rem(home_row(me) + grp, 2) == 1)
        def _():
            wait(transit, 16 * CAP, pass_sem)

        wait(ids_out, N_OWN, ids_send_sem)

    got = exact(dot, mass_in[:, 0, :], rank_ref[...])
    mass = jnp.sum(got * rowhot_ref[...], axis=0, keepdims=True)
    score = jnp.broadcast_to(jnp.log(mass) - SHARPNESS, (16, R_DEV))
    dup_ref[...] = exact(dot_t, score, target_ref[...])[0:1].reshape(R_DEV)


def local(embeddings, cluster_ids, owner_map, source_order):
    vmem = pl.BlockSpec(memory_space=pltpu.VMEM)
    dma = pltpu.SemaphoreType.DMA
    dup, centroids = pl.pallas_call(
        kernel,
        out_shape=(jax.ShapeDtypeStruct((R_DEV,), F32), jax.ShapeDtypeStruct((CL_OWN, D), F32)),
        in_specs=[pl.BlockSpec(memory_space=pl.ANY)] + [vmem] * 3,
        out_specs=(vmem, vmem),
        scratch_shapes=[
            pltpu.VMEM((SLOTS, D), F32),
            pltpu.VMEM((N_OWN, 1, 128), F32),
            pltpu.VMEM((MSGS * CAP, D), F32),
            pltpu.VMEM((MSGS, 1, 128), F32),
            pltpu.VMEM((MSGS * CAP, D), BF16),
            pltpu.VMEM((MSGS * CAP, 128), F32),
            pltpu.VMEM((8, MSGS * CAP), F32),
            pltpu.VMEM((MSGS * CAP, 128), F32),
            pltpu.VMEM((8, MSGS * CAP), F32),
            pltpu.VMEM((MSGS * CAP, 128), F32),
            pltpu.VMEM((8, MSGS * CAP), F32),
            pltpu.VMEM((CL_OWN, D), F32),
            pltpu.VMEM((N_OWN, R_DEV), F32),
            pltpu.VMEM((128, R_DEV), BF16),
            pltpu.VMEM((MSGS, 1, 128), F32),
            pltpu.VMEM((N_OWN, 1, 128), F32),
            pltpu.VMEM((CL_OWN, D), F32),
            pltpu.VMEM((16 * CAP, D), F32),
            pltpu.VMEM((R_DEV, D), F32),
            pltpu.VMEM((R_DEV, R_DEV), BF16),
            dma((N_OWN,)), dma((N_OWN,)), dma, dma, dma((CHUNKS,)), dma((CHUNKS,)), dma((3,)), dma, dma, dma((3,)), dma,
        ],
        compiler_params=pltpu.CompilerParams(collective_id=0, has_side_effects=True, vmem_limit_bytes=60 << 20),
        name="owner_gather",
    )(
        embeddings,
        cluster_ids,
        owner_map,
        source_order,
    )
    return dup, centroids


def solution(mesh):
    placed = (P(("grp", "own"), None), P(("grp", "own")), P(), P(("grp", "own")))
    return jax.shard_map(
        local,
        mesh=mesh,
        in_specs=placed,
        out_specs=(P(("grp", "own")), P("own", None)),
        check_vma=False,
    )
```

```python
import functools

import jax
import jax.numpy as jnp
from jax import lax
from jax.experimental import pallas as pl
from jax.experimental.pallas import tpu as pltpu
from jax.sharding import PartitionSpec as P

MESH = pl.DeviceIdType.MESH
F32 = jnp.float32
BF16 = jnp.bfloat16

N_GRP = 4
N_OWN = 32
D = 768
R_DEV = 768
CLUSTERS = 512
CL_OWN = 16
CAP = 48
SLOTS = N_OWN * CAP
MSGS = N_GRP * N_OWN
CHUNK_MSGS = 16
CHUNK = CHUNK_MSGS * CAP
CHUNKS = MSGS // CHUNK_MSGS
SHARPNESS = 6.0
RELAYED = (4, 7)
SELF = 31
SELF_CHUNK = 6
WINDOW = 9
PACKS = 4
PART = 256
LAG = 5


def hot(condition):
    return jnp.where(condition, 1.0, 0.0).astype(BF16)


def iota(shape, dim):
    return lax.broadcasted_iota(jnp.int32, shape, dim)


def by_48(n):
    return (n * 1366) >> 16


def dot(a, b):
    return lax.dot_general(a, b, (((1,), (0,)), ((), ())), preferred_element_type=F32)


def dot_t(a, b):
    return lax.dot_general(a, b, (((1,), (1,)), ((), ())), preferred_element_type=F32)


def split3(a):
    high = a.astype(BF16)
    rest = a - high.astype(F32)
    middle = rest.astype(BF16)
    low = (rest - middle.astype(F32)).astype(BF16)
    return high, middle, low


def exact(product, a, b):
    rows = a.shape[0]
    out = product(jnp.concatenate(split3(a), axis=0), b)
    return out[:rows] + (out[rows : 2 * rows] + out[2 * rows :])


def home_row(owner):
    x, z, core = owner // 8, lax.rem(owner // 2, 4), lax.rem(owner, 2)
    return lax.rem(x + z, 2) + 2 * core


def partner(me, i, back=False):
    a, b, c = lax.rem(i, 4), lax.rem(i // 4, 4), i // 16
    dx = lax.rem(10 - a - b, 4)
    dz = jnp.where(a == 0, 2, jnp.where(a == 1, 1, jnp.where(a == 2, 3, 0)))
    dc = lax.rem(a + c, 2)
    if back:
        dx, dz = 4 - dx, 4 - dz
    x, z, core = me // 8, lax.rem(me // 2, 4), lax.rem(me, 2)
    return lax.rem(x + dx, 4) * 8 + lax.rem(z + dz, 4) * 2 + lax.rem(core + dc, 2)


def step_to(me, owner):
    dx = lax.rem(owner // 8 - me // 8 + 8, 4)
    dz = lax.rem(lax.rem(owner // 2, 4) - lax.rem(me // 2, 4) + 4, 4)
    dc = lax.rem(owner + me, 2)
    a = jnp.where(dz == 2, 0, jnp.where(dz == 1, 1, jnp.where(dz == 3, 2, 3)))
    return a + 4 * lax.rem(18 - a - dx, 4) + 16 * lax.rem(dc + a, 2)


def in_transit(source, grp, owner):
    z_step = lax.rem(owner // 2 - source // 2 + 2 * N_OWN, 4)
    y_step = lax.rem(home_row(owner) - grp + 4, 4)
    via = ((y_step == 1) & (z_step >= 2)) | ((y_step == 3) & (z_step >= 1) & (z_step <= 2))
    late = jnp.where(y_step == 1, z_step - 2, z_step - 1)
    return via, late * 8 + source // 8 * 2 + lax.rem(source, 2)


def place_of(i, y_step):
    group, a = i // 4, lax.rem(i, 4)
    via = ((a == 0) & (lax.rem(y_step, 2) == 1)) | ((a == 1) & (y_step == 3)) | ((a == 2) & (y_step == 1))
    early = jnp.where(
        a == 0, y_step // 2, jnp.where(a == 1, 2 + y_step, jnp.where(a == 2, 5 + jnp.maximum(y_step - 1, 0), 8 + y_step))
    )
    n = jnp.where(via, 4 * group + jnp.where(a == 0, y_step // 2, a + 1), 12 * group + early)
    k = n // CHUNK_MSGS
    late = jnp.where(k == 0, RELAYED[0], RELAYED[1])
    k = jnp.where(via, late, k + jnp.where(k >= RELAYED[0], 1, 0))
    return k * CHUNK_MSGS + lax.rem(n, CHUNK_MSGS)


def messages():
    early, late = [], []
    for i in range(N_OWN):
        for y_step in range(N_GRP):
            via = (i % 4, y_step) in ((0, 1), (0, 3), (1, 3), (2, 1))
            (late if via else early).append((i, y_step))
    first = RELAYED[0] * CHUNK_MSGS
    return early[:first] + late[:CHUNK_MSGS] + early[first:] + late[CHUNK_MSGS:]


def kernel(
    x_ref, cid_ref, map_ref, order_ref, dup_ref, cen_ref,
    packed, ids_out, land, ids_in, unit, row_acc, col_acc, id_col, id_row, scale_col, scale_row, sums, rowhot_ref, rank_ref,
    mass_out, mass_in, cen_in, transit, x_held, target_ref,
    send_sem, transit_sem, pass_sem, ids_send_sem, recv_sem, ids_recv_sem, local_sem, back_send_sem, back_recv_sem, cen_send_sem, cen_recv_sem,
):
    me, grp = lax.axis_index("own"), lax.axis_index("grp")
    home = grp == home_row(me)

    barrier = pltpu.get_barrier_semaphore()

    def tell(grp_to, own_to):
        pl.semaphore_signal(barrier, inc=1, device_id=(grp_to, own_to), device_id_type=MESH)

    def tell_home(o, _):
        to = home_row(o)

        @pl.when(jnp.logical_not(home & (o == me)))
        def _():
            tell(to, o)

        return 0

    lax.fori_loop(0, N_OWN, tell_home, 0)

    @pl.when(home)
    def _():
        def tell_others(m, _):
            @pl.when(home_row(m // N_GRP) != lax.rem(m, N_GRP))
            def _():
                tell(lax.rem(m, N_GRP), m // N_GRP)

            return 0

        lax.fori_loop(0, MSGS, tell_others, 0)

    @pl.when(jnp.logical_not(home))
    def _():
        def tell_senders(o, _):
            @pl.when(in_transit(o, grp, me)[0] & (home_row(o) != grp))
            def _():
                tell(grp, o)

            return 0

        lax.fori_loop(0, N_OWN, tell_senders, 0)

    x_copy = pltpu.make_async_copy(x_ref, x_held, local_sem.at[1])
    x_copy.start()

    owner_hot = hot(iota((N_OWN, CLUSTERS), 0) == map_ref[...].reshape(1, CLUSTERS))
    earlier = hot(iota((CLUSTERS, CLUSTERS), 0) < iota((CLUSTERS, CLUSTERS), 1))
    before = dot(owner_hot, earlier)
    place = jnp.sum(owner_hot.astype(F32) * before, axis=0, keepdims=True)
    table = jnp.concatenate([owner_hot, jnp.broadcast_to(place, (16, CLUSTERS)).astype(BF16)], axis=0)
    looked_up = dot(table, hot(iota((CLUSTERS, R_DEV), 0) == cid_ref[...].reshape(1, R_DEV)))
    row_hot, row_place = looked_up[:N_OWN], looked_up[N_OWN : N_OWN + 1]
    ahead = hot(iota((R_DEV, R_DEV), 0) < iota((R_DEV, R_DEV), 1))
    rank = jnp.sum(row_hot * dot(row_hot.astype(BF16), ahead), axis=0, keepdims=True)
    owner = jnp.sum(row_hot * iota((N_OWN, R_DEV), 0).astype(F32), axis=0, keepdims=True)
    rank = rank.astype(jnp.int32)
    slot = step_to(me, owner.astype(jnp.int32)) * CAP + rank
    rank_hot = hot(iota((128, R_DEV), 0) == rank)
    rowhot_ref[...] = row_hot
    rank_ref[...] = rank_hot
    ids = dot_t((row_hot * (row_place + 1.0)).astype(BF16), rank_hot) - 1.0
    ids_out[:, 0, :] = ids

    x_copy.wait()
    x = x_held[...]
    u = x * lax.rsqrt(jnp.sum(x * x, axis=1, keepdims=True) + 1e-06)
    high = u.astype(BF16)
    low = (u - high.astype(F32)).astype(BF16)
    block = SLOTS // PACKS

    def pack(k):
        pick = hot(iota((block, R_DEV), 0) + k * block == slot)
        packed[pl.ds(k * block, block)] = dot(pick, high) + dot(pick, low)

    pack(0)

    @pl.when(home)
    def _():
        pl.semaphore_wait(barrier, MSGS - 1)

    @pl.when(jnp.logical_not(home))
    def _():
        pl.semaphore_wait(barrier, N_OWN + 8)

    def at_slot(m):
        return pl.ds(pl.multiple_of(m * CAP, CAP), CAP)

    def send(i):
        o = partner(me, i)
        to = home_row(o)
        here = (o == me) & (to == grp)
        via, place = in_transit(me, grp, o)
        m = place_of(i, lax.rem(to - grp + N_GRP, N_GRP))
        part = m // CHUNK_MSGS

        @pl.when(jnp.logical_not(here))
        def _():
            pltpu.make_async_remote_copy(
                src_ref=ids_out.at[o], dst_ref=ids_in.at[m], send_sem=ids_send_sem,
                recv_sem=ids_recv_sem.at[part], device_id=(to, o), device_id_type=MESH,
            ).start()

        @pl.when(jnp.logical_not(here | via))
        def _():
            pltpu.make_async_remote_copy(
                src_ref=packed.at[at_slot(i)], dst_ref=land.at[at_slot(m)], send_sem=send_sem.at[i],
                recv_sem=recv_sem.at[part], device_id=(to, o), device_id_type=MESH,
            ).start()

        @pl.when(via)
        def _():
            pltpu.make_async_remote_copy(
                src_ref=packed.at[at_slot(i)], dst_ref=transit.at[at_slot(place)], send_sem=send_sem.at[i],
                recv_sem=transit_sem.at[i], device_id=(grp, o), device_id_type=MESH,
            ).start()

        @pl.when(here)
        def _():
            pltpu.make_async_copy(ids_out.at[o], ids_in.at[m], local_sem.at[0]).start()
            pltpu.make_async_copy(packed.at[at_slot(i)], land.at[at_slot(m)], send_sem.at[i]).start()

    def pass_on(i):
        source = partner(me, i, back=True)
        via, place = in_transit(source, grp, me)

        @pl.when(via)
        def _():
            m = place_of(i, lax.rem(home_row(me) - grp + N_GRP, N_GRP))
            here = transit.at[at_slot(place)]
            pltpu.make_async_copy(here, here, transit_sem.at[i]).wait()
            pltpu.make_async_remote_copy(
                src_ref=here, dst_ref=land.at[at_slot(m)], send_sem=pass_sem,
                recv_sem=recv_sem.at[m // CHUNK_MSGS], device_id=(home_row(me), me), device_id_type=MESH,
            ).start()

    def sent(i):
        pltpu.make_async_copy(packed.at[at_slot(0)], packed.at[at_slot(0)], send_sem.at[i]).wait()

    def step(i, _):
        @pl.when(jnp.logical_not(home) & (i >= WINDOW) & (i < N_OWN + WINDOW))
        def _():
            sent(i - WINDOW)

        @pl.when(i < N_OWN)
        def _():
            send(i)

        @pl.when((i >= LAG) & (i < N_OWN + LAG))
        def _():
            pass_on(i - LAG)

        return 0

    for k in range(PACKS):
        if k:
            pack(k)
        group = N_OWN // PACKS
        lax.fori_loop(k * group, (k + 1) * group, step, 0)
    lax.fori_loop(N_OWN, N_OWN + max(WINDOW, LAG), step, 0)

    def wait(ref, count, sem):
        pltpu.make_async_copy(ref.at[pl.ds(0, count)], ref.at[pl.ds(0, count)], sem).wait()

    target_ref[...] = hot(iota((R_DEV, R_DEV), 0) == order_ref[...].reshape(1, R_DEV))
    cols = iota((128, CHUNK), 1)
    spread = hot(cols - CAP * by_48(cols) == iota((128, CHUNK), 0))
    mine = by_48(iota((CHUNK_MSGS, CHUNK), 1)) == iota((CHUNK_MSGS, CHUNK), 0)

    def weigh(rows, right, width, only_rows):
        scores = dot_t(unit[rows], unit[pl.ds(right, width)])
        left_ids, left_scale, total = id_col[rows], scale_col[rows], row_acc[rows]
        columns = []
        for t in range(width // 128):
            lanes = pl.ds(right + t * 128, 128)
            weights = jnp.exp(scores[:, t * 128 : (t + 1) * 128] * left_scale * scale_row[0:1, lanes])
            weights = jnp.where(left_ids == id_row[0:1, lanes], weights, 0.0)
            total = total + weights
            if t < only_rows:
                columns.append(jnp.sum(weights.reshape(PART // 8, 8, 128), axis=0))
        row_acc[rows] = total
        return columns

    def add_columns(right, columns):
        for t, column in enumerate(columns):
            col_acc[:, pl.ds(right + t * 128, 128)] += column

    def pair(a, b):
        left = pl.multiple_of(a * CHUNK, CHUNK)
        right = pl.multiple_of(b * CHUNK, CHUNK)
        parts = [weigh(pl.ds(left + r * PART, PART), right, CHUNK, CHUNK // 128) for r in range(CHUNK // PART)]
        add_columns(right, [sum(each) for each in zip(*parts)])

    def inner(a):
        left = pl.multiple_of(a * CHUNK, CHUNK)
        for r in range(CHUNK // PART):
            add_columns(left, weigh(pl.ds(left + r * PART, PART), left, (r + 1) * PART, r * PART // 128))

    @pl.when(home)
    def _():
        sums[...] = jnp.zeros_like(sums)
        row_acc[...] = jnp.zeros_like(row_acc)
        col_acc[...] = jnp.zeros_like(col_acc)
        wait(ids_out, 1, local_sem.at[0])
        sent(SELF)

        def prepare(a):
            @pl.when(a == SELF_CHUNK)
            def _():
                wait(ids_in, CHUNK_MSGS - 1, ids_recv_sem.at[SELF_CHUNK])
                wait(land, CHUNK - CAP, recv_sem.at[SELF_CHUNK])

            @pl.when(a != SELF_CHUNK)
            def _():
                wait(ids_in, CHUNK_MSGS, ids_recv_sem.at[a])
                wait(land, CHUNK, recv_sem.at[a])

            base = pl.multiple_of(a * CHUNK, CHUNK)
            rows = pl.ds(base, CHUNK)
            got = land[rows]
            high = got.astype(BF16)
            unit[rows] = high
            wide = high.astype(F32)
            low = (got - wide).astype(BF16)
            kept = jnp.sum(wide * wide, axis=1, keepdims=True)
            off = jnp.sqrt(jnp.sum(got * got, axis=1, keepdims=True) / jnp.maximum(kept, 1e-30))
            off = jnp.where(kept > 0.0, off - 1.0, 0.0)
            off = jnp.broadcast_to(off, (CHUNK, 128))
            scale_col[rows] = SHARPNESS + SHARPNESS * off
            scale_row[:, rows] = 1.0 + dot_t(hot(iota((8, 128), 1) == 0), off.astype(BF16))
            ids = ids_in[pl.ds(a * CHUNK_MSGS, CHUNK_MSGS), 0, :].astype(BF16)
            in_row = jnp.where(mine, dot(ids, spread), 0.0).astype(BF16)
            row = dot(jnp.ones((8, CHUNK_MSGS), BF16), in_row)
            id_row[:, rows] = row
            at = iota((CHUNK, 128), 0)
            picked = dot(hot(by_48(iota((CHUNK, CHUNK_MSGS), 0)) == iota((CHUNK, CHUNK_MSGS), 1)), ids)
            picked = jnp.where(at - CAP * by_48(at) == iota((CHUNK, 128), 1), picked, 0.0).astype(BF16)
            id_col[rows] = dot(picked, jnp.ones((128, 128), BF16))
            member = hot(iota((CL_OWN, CHUNK), 0).astype(F32) == row[0:1])
            sums[...] += dot(member, high) + dot(member, low)

        def chunk(a, _):
            prepare(a)
            lax.fori_loop(0, a, lambda b, _: (pair(a, b), 0)[1], 0)
            inner(a)
            return 0

        last = CHUNKS - 1
        lax.fori_loop(0, last, chunk, 0)
        prepare(last)
        total = sums[...]
        cen_ref[...] = total * lax.rsqrt(jnp.mean(total * total, axis=1, keepdims=True) + 1e-06)
        for k in range(1, N_GRP):
            pltpu.make_async_remote_copy(
                src_ref=cen_ref, dst_ref=cen_in, send_sem=cen_send_sem.at[k - 1], recv_sem=cen_recv_sem,
                device_id=(lax.rem(grp + k, N_GRP), me), device_id_type=MESH,
            ).start()

        order = messages()

        def give_back(a):
            rows = pl.ds(a * CHUNK, CHUNK)
            part = row_acc[rows]
            high, middle, low = split3(part)
            ones = jnp.ones((8, 128), BF16)
            mass = dot_t(ones, high) + (dot_t(ones, middle) + dot_t(ones, low))
            mass = mass[0:1] + jnp.sum(col_acc[:, rows], axis=0, keepdims=True)
            back = exact(dot_t, jnp.where(mine, mass, 0.0), spread)
            mass_out[pl.ds(a * CHUNK_MSGS, CHUNK_MSGS), 0, :] = back
            for j in range(CHUNK_MSGS):
                i, y_step = order[a * CHUNK_MSGS + j]
                to_grp = lax.rem(grp + N_GRP - y_step, N_GRP)
                to = partner(me, i, back=True)
                here = (i, y_step) == (SELF, 0)

                block = mass_out.at[a * CHUNK_MSGS + j]
                if here:
                    pltpu.make_async_copy(block, mass_in.at[me], local_sem.at[2]).start()
                else:
                    pltpu.make_async_remote_copy(
                        src_ref=block, dst_ref=mass_in.at[me], send_sem=back_send_sem,
                        recv_sem=back_recv_sem, device_id=(to_grp, to), device_id_type=MESH,
                    ).start()

        lax.fori_loop(0, last, lambda b, _: (pair(last, b), 0)[1], 0)
        inner(last)
        for a in range(CHUNKS):
            give_back(a)

        for k in range(1, N_GRP):
            pltpu.make_async_copy(cen_ref, cen_ref, cen_send_sem.at[k - 1]).wait()
        wait(mass_out, MSGS - 1, back_send_sem)
        wait(mass_out, 1, local_sem.at[2])
        wait(mass_in, N_OWN - 1, back_recv_sem)
        lax.fori_loop(0, N_OWN - 1, lambda i, _: (sent(lax.rem(SELF + 1 + i, N_OWN)), 0)[1], 0)
        wait(ids_out, N_OWN - 1, ids_send_sem)

    @pl.when(jnp.logical_not(home))
    def _():
        pltpu.make_async_copy(cen_in, cen_in, cen_recv_sem).wait()
        cen_ref[...] = cen_in[...]
        wait(mass_in, N_OWN, back_recv_sem)

        @pl.when(lax.rem(home_row(me) + grp, 2) == 1)
        def _():
            wait(transit, 16 * CAP, pass_sem)

        wait(ids_out, N_OWN, ids_send_sem)

    got = exact(dot, mass_in[:, 0, :], rank_ref[...])
    mass = jnp.sum(got * rowhot_ref[...], axis=0, keepdims=True)
    score = jnp.broadcast_to(jnp.log(mass) - SHARPNESS, (16, R_DEV))
    dup_ref[...] = exact(dot_t, score, target_ref[...])[0:1].reshape(R_DEV)


def local(embeddings, cluster_ids, owner_map, source_order):
    vmem = pl.BlockSpec(memory_space=pltpu.VMEM)
    dma = pltpu.SemaphoreType.DMA
    dup, centroids = pl.pallas_call(
        kernel,
        out_shape=(jax.ShapeDtypeStruct((R_DEV,), F32), jax.ShapeDtypeStruct((CL_OWN, D), F32)),
        in_specs=[pl.BlockSpec(memory_space=pl.ANY)] + [vmem] * 3,
        out_specs=(vmem, vmem),
        scratch_shapes=[
            pltpu.VMEM((SLOTS, D), F32),
            pltpu.VMEM((N_OWN, 1, 128), F32),
            pltpu.VMEM((MSGS * CAP, D), F32),
            pltpu.VMEM((MSGS, 1, 128), F32),
            pltpu.VMEM((MSGS * CAP, D), BF16),
            pltpu.VMEM((MSGS * CAP, 128), F32),
            pltpu.VMEM((8, MSGS * CAP), F32),
            pltpu.VMEM((MSGS * CAP, 128), F32),
            pltpu.VMEM((8, MSGS * CAP), F32),
            pltpu.VMEM((MSGS * CAP, 128), F32),
            pltpu.VMEM((8, MSGS * CAP), F32),
            pltpu.VMEM((CL_OWN, D), F32),
            pltpu.VMEM((N_OWN, R_DEV), F32),
            pltpu.VMEM((128, R_DEV), BF16),
            pltpu.VMEM((MSGS, 1, 128), F32),
            pltpu.VMEM((N_OWN, 1, 128), F32),
            pltpu.VMEM((CL_OWN, D), F32),
            pltpu.VMEM((16 * CAP, D), F32),
            pltpu.VMEM((R_DEV, D), F32),
            pltpu.VMEM((R_DEV, R_DEV), BF16),
            dma((N_OWN,)), dma((N_OWN,)), dma, dma, dma((CHUNKS,)), dma((CHUNKS,)), dma((3,)), dma, dma, dma((3,)), dma,
        ],
        compiler_params=pltpu.CompilerParams(collective_id=0, has_side_effects=True, vmem_limit_bytes=60 << 20),
        name="owner_gather",
    )(
        embeddings,
        cluster_ids,
        owner_map,
        source_order,
    )
    return dup, centroids


def solution(mesh):
    placed = (P(("grp", "own"), None), P(("grp", "own")), P(), P(("grp", "own")))
    return jax.shard_map(
        local,
        mesh=mesh,
        in_specs=placed,
        out_specs=(P(("grp", "own")), P("own", None)),
        check_vma=False,
    )
```

```python
import functools

import jax
import jax.numpy as jnp
from jax import lax
from jax.experimental import pallas as pl
from jax.experimental.pallas import tpu as pltpu
from jax.sharding import PartitionSpec as P

MESH = pl.DeviceIdType.MESH
F32 = jnp.float32
BF16 = jnp.bfloat16

N_GRP = 4
N_OWN = 32
D = 768
R_DEV = 768
CLUSTERS = 512
CL_OWN = 16
CAP = 48
SLOTS = N_OWN * CAP
MSGS = N_GRP * N_OWN
CHUNK_MSGS = 16
CHUNK = CHUNK_MSGS * CAP
CHUNKS = MSGS // CHUNK_MSGS
SHARPNESS = 6.0
RELAYED = (4, 7)
SELF = 31
SELF_CHUNK = 6
WINDOW = 9
PACKS = 4
PART = 256
LAG = 4


def hot(condition):
    return jnp.where(condition, 1.0, 0.0).astype(BF16)


def iota(shape, dim):
    return lax.broadcasted_iota(jnp.int32, shape, dim)


def by_48(n):
    return (n * 1366) >> 16


def dot(a, b):
    return lax.dot_general(a, b, (((1,), (0,)), ((), ())), preferred_element_type=F32)


def dot_t(a, b):
    return lax.dot_general(a, b, (((1,), (1,)), ((), ())), preferred_element_type=F32)


def split3(a):
    high = a.astype(BF16)
    rest = a - high.astype(F32)
    middle = rest.astype(BF16)
    low = (rest - middle.astype(F32)).astype(BF16)
    return high, middle, low


def exact(product, a, b):
    rows = a.shape[0]
    out = product(jnp.concatenate(split3(a), axis=0), b)
    return out[:rows] + (out[rows : 2 * rows] + out[2 * rows :])


def home_row(owner):
    x, z, core = owner // 8, lax.rem(owner // 2, 4), lax.rem(owner, 2)
    return lax.rem(x + z, 2) + 2 * core


def partner(me, i, back=False):
    a, b, c = lax.rem(i, 4), lax.rem(i // 4, 4), i // 16
    dx = lax.rem(10 - a - b, 4)
    dz = jnp.where(a == 0, 2, jnp.where(a == 1, 1, jnp.where(a == 2, 3, 0)))
    dc = lax.rem(a + c, 2)
    if back:
        dx, dz = 4 - dx, 4 - dz
    x, z, core = me // 8, lax.rem(me // 2, 4), lax.rem(me, 2)
    return lax.rem(x + dx, 4) * 8 + lax.rem(z + dz, 4) * 2 + lax.rem(core + dc, 2)


def step_to(me, owner):
    dx = lax.rem(owner // 8 - me // 8 + 8, 4)
    dz = lax.rem(lax.rem(owner // 2, 4) - lax.rem(me // 2, 4) + 4, 4)
    dc = lax.rem(owner + me, 2)
    a = jnp.where(dz == 2, 0, jnp.where(dz == 1, 1, jnp.where(dz == 3, 2, 3)))
    return a + 4 * lax.rem(18 - a - dx, 4) + 16 * lax.rem(dc + a, 2)


def in_transit(source, grp, owner):
    z_step = lax.rem(owner // 2 - source // 2 + 2 * N_OWN, 4)
    y_step = lax.rem(home_row(owner) - grp + 4, 4)
    via = ((y_step == 1) & (z_step >= 2)) | ((y_step == 3) & (z_step >= 1) & (z_step <= 2))
    late = jnp.where(y_step == 1, z_step - 2, z_step - 1)
    return via, late * 8 + source // 8 * 2 + lax.rem(source, 2)


def place_of(i, y_step):
    group, a = i // 4, lax.rem(i, 4)
    via = ((a == 0) & (lax.rem(y_step, 2) == 1)) | ((a == 1) & (y_step == 3)) | ((a == 2) & (y_step == 1))
    early = jnp.where(
        a == 0, y_step // 2, jnp.where(a == 1, 2 + y_step, jnp.where(a == 2, 5 + jnp.maximum(y_step - 1, 0), 8 + y_step))
    )
    n = jnp.where(via, 4 * group + jnp.where(a == 0, y_step // 2, a + 1), 12 * group + early)
    k = n // CHUNK_MSGS
    late = jnp.where(k == 0, RELAYED[0], RELAYED[1])
    k = jnp.where(via, late, k + jnp.where(k >= RELAYED[0], 1, 0))
    return k * CHUNK_MSGS + lax.rem(n, CHUNK_MSGS)


def messages():
    early, late = [], []
    for i in range(N_OWN):
        for y_step in range(N_GRP):
            via = (i % 4, y_step) in ((0, 1), (0, 3), (1, 3), (2, 1))
            (late if via else early).append((i, y_step))
    first = RELAYED[0] * CHUNK_MSGS
    return early[:first] + late[:CHUNK_MSGS] + early[first:] + late[CHUNK_MSGS:]


def kernel(
    x_ref, cid_ref, map_ref, order_ref, dup_ref, cen_ref,
    packed, ids_out, land, ids_in, unit, row_acc, col_acc, id_col, id_row, scale_col, scale_row, sums, rowhot_ref, rank_ref,
    mass_out, mass_in, cen_in, transit, x_held, target_ref,
    send_sem, transit_sem, pass_sem, ids_send_sem, recv_sem, ids_recv_sem, local_sem, back_send_sem, back_recv_sem, cen_send_sem, cen_recv_sem,
):
    me, grp = lax.axis_index("own"), lax.axis_index("grp")
    home = grp == home_row(me)

    barrier = pltpu.get_barrier_semaphore()

    def tell(grp_to, own_to):
        pl.semaphore_signal(barrier, inc=1, device_id=(grp_to, own_to), device_id_type=MESH)

    def tell_home(o, _):
        to = home_row(o)

        @pl.when(jnp.logical_not(home & (o == me)))
        def _():
            tell(to, o)

        return 0

    lax.fori_loop(0, N_OWN, tell_home, 0)

    @pl.when(home)
    def _():
        def tell_others(m, _):
            @pl.when(home_row(m // N_GRP) != lax.rem(m, N_GRP))
            def _():
                tell(lax.rem(m, N_GRP), m // N_GRP)

            return 0

        lax.fori_loop(0, MSGS, tell_others, 0)

    @pl.when(jnp.logical_not(home))
    def _():
        def tell_senders(o, _):
            @pl.when(in_transit(o, grp, me)[0] & (home_row(o) != grp))
            def _():
                tell(grp, o)

            return 0

        lax.fori_loop(0, N_OWN, tell_senders, 0)

    x_copy = pltpu.make_async_copy(x_ref, x_held, local_sem.at[1])
    x_copy.start()

    owner_hot = hot(iota((N_OWN, CLUSTERS), 0) == map_ref[...].reshape(1, CLUSTERS))
    earlier = hot(iota((CLUSTERS, CLUSTERS), 0) < iota((CLUSTERS, CLUSTERS), 1))
    before = dot(owner_hot, earlier)
    place = jnp.sum(owner_hot.astype(F32) * before, axis=0, keepdims=True)
    table = jnp.concatenate([owner_hot, jnp.broadcast_to(place, (16, CLUSTERS)).astype(BF16)], axis=0)
    looked_up = dot(table, hot(iota((CLUSTERS, R_DEV), 0) == cid_ref[...].reshape(1, R_DEV)))
    row_hot, row_place = looked_up[:N_OWN], looked_up[N_OWN : N_OWN + 1]
    ahead = hot(iota((R_DEV, R_DEV), 0) < iota((R_DEV, R_DEV), 1))
    rank = jnp.sum(row_hot * dot(row_hot.astype(BF16), ahead), axis=0, keepdims=True)
    owner = jnp.sum(row_hot * iota((N_OWN, R_DEV), 0).astype(F32), axis=0, keepdims=True)
    rank = rank.astype(jnp.int32)
    slot = step_to(me, owner.astype(jnp.int32)) * CAP + rank
    rank_hot = hot(iota((128, R_DEV), 0) == rank)
    rowhot_ref[...] = row_hot
    rank_ref[...] = rank_hot
    ids = dot_t((row_hot * (row_place + 1.0)).astype(BF16), rank_hot) - 1.0
    ids_out[:, 0, :] = ids

    x_copy.wait()
    x = x_held[...]
    u = x * lax.rsqrt(jnp.sum(x * x, axis=1, keepdims=True) + 1e-06)
    high = u.astype(BF16)
    low = (u - high.astype(F32)).astype(BF16)
    block = SLOTS // PACKS

    def pack(k):
        pick = hot(iota((block, R_DEV), 0) + k * block == slot)
        packed[pl.ds(k * block, block)] = dot(pick, high) + dot(pick, low)

    pack(0)

    @pl.when(home)
    def _():
        pl.semaphore_wait(barrier, MSGS - 1)

    @pl.when(jnp.logical_not(home))
    def _():
        pl.semaphore_wait(barrier, N_OWN + 8)

    def at_slot(m):
        return pl.ds(pl.multiple_of(m * CAP, CAP), CAP)

    def send(i):
        o = partner(me, i)
        to = home_row(o)
        here = (o == me) & (to == grp)
        via, place = in_transit(me, grp, o)
        m = place_of(i, lax.rem(to - grp + N_GRP, N_GRP))
        part = m // CHUNK_MSGS

        @pl.when(jnp.logical_not(here))
        def _():
            pltpu.make_async_remote_copy(
                src_ref=ids_out.at[o], dst_ref=ids_in.at[m], send_sem=ids_send_sem,
                recv_sem=ids_recv_sem.at[part], device_id=(to, o), device_id_type=MESH,
            ).start()

        @pl.when(jnp.logical_not(here | via))
        def _():
            pltpu.make_async_remote_copy(
                src_ref=packed.at[at_slot(i)], dst_ref=land.at[at_slot(m)], send_sem=send_sem.at[i],
                recv_sem=recv_sem.at[part], device_id=(to, o), device_id_type=MESH,
            ).start()

        @pl.when(via)
        def _():
            pltpu.make_async_remote_copy(
                src_ref=packed.at[at_slot(i)], dst_ref=transit.at[at_slot(place)], send_sem=send_sem.at[i],
                recv_sem=transit_sem.at[i], device_id=(grp, o), device_id_type=MESH,
            ).start()

        @pl.when(here)
        def _():
            pltpu.make_async_copy(ids_out.at[o], ids_in.at[m], local_sem.at[0]).start()
            pltpu.make_async_copy(packed.at[at_slot(i)], land.at[at_slot(m)], send_sem.at[i]).start()

    def pass_on(i):
        source = partner(me, i, back=True)
        via, place = in_transit(source, grp, me)

        @pl.when(via)
        def _():
            m = place_of(i, lax.rem(home_row(me) - grp + N_GRP, N_GRP))
            here = transit.at[at_slot(place)]
            pltpu.make_async_copy(here, here, transit_sem.at[i]).wait()
            pltpu.make_async_remote_copy(
                src_ref=here, dst_ref=land.at[at_slot(m)], send_sem=pass_sem,
                recv_sem=recv_sem.at[m // CHUNK_MSGS], device_id=(home_row(me), me), device_id_type=MESH,
            ).start()

    def sent(i):
        pltpu.make_async_copy(packed.at[at_slot(0)], packed.at[at_slot(0)], send_sem.at[i]).wait()

    def step(i, _):
        @pl.when(jnp.logical_not(home) & (i >= WINDOW) & (i < N_OWN + WINDOW))
        def _():
            sent(i - WINDOW)

        @pl.when(i < N_OWN)
        def _():
            send(i)

        @pl.when((i >= LAG) & (i < N_OWN + LAG))
        def _():
            pass_on(i - LAG)

        return 0

    for k in range(PACKS):
        if k:
            pack(k)
        group = N_OWN // PACKS
        lax.fori_loop(k * group, (k + 1) * group, step, 0)
    lax.fori_loop(N_OWN, N_OWN + max(WINDOW, LAG), step, 0)

    def wait(ref, count, sem):
        pltpu.make_async_copy(ref.at[pl.ds(0, count)], ref.at[pl.ds(0, count)], sem).wait()

    target_ref[...] = hot(iota((R_DEV, R_DEV), 0) == order_ref[...].reshape(1, R_DEV))
    cols = iota((128, CHUNK), 1)
    spread = hot(cols - CAP * by_48(cols) == iota((128, CHUNK), 0))
    mine = by_48(iota((CHUNK_MSGS, CHUNK), 1)) == iota((CHUNK_MSGS, CHUNK), 0)

    def weigh(rows, right, width, only_rows):
        scores = dot_t(unit[rows], unit[pl.ds(right, width)])
        left_ids, left_scale, total = id_col[rows], scale_col[rows], row_acc[rows]
        columns = []
        for t in range(width // 128):
            lanes = pl.ds(right + t * 128, 128)
            weights = jnp.exp(scores[:, t * 128 : (t + 1) * 128] * left_scale * scale_row[0:1, lanes])
            weights = jnp.where(left_ids == id_row[0:1, lanes], weights, 0.0)
            total = total + weights
            if t < only_rows:
                columns.append(jnp.sum(weights.reshape(PART // 8, 8, 128), axis=0))
        row_acc[rows] = total
        return columns

    def add_columns(right, columns):
        for t, column in enumerate(columns):
            col_acc[:, pl.ds(right + t * 128, 128)] += column

    def pair(a, b):
        left = pl.multiple_of(a * CHUNK, CHUNK)
        right = pl.multiple_of(b * CHUNK, CHUNK)
        parts = [weigh(pl.ds(left + r * PART, PART), right, CHUNK, CHUNK // 128) for r in range(CHUNK // PART)]
        add_columns(right, [sum(each) for each in zip(*parts)])

    def inner(a):
        left = pl.multiple_of(a * CHUNK, CHUNK)
        for r in range(CHUNK // PART):
            add_columns(left, weigh(pl.ds(left + r * PART, PART), left, (r + 1) * PART, r * PART // 128))

    @pl.when(home)
    def _():
        sums[...] = jnp.zeros_like(sums)
        row_acc[...] = jnp.zeros_like(row_acc)
        col_acc[...] = jnp.zeros_like(col_acc)
        wait(ids_out, 1, local_sem.at[0])
        sent(SELF)

        def prepare(a):
            @pl.when(a == SELF_CHUNK)
            def _():
                wait(ids_in, CHUNK_MSGS - 1, ids_recv_sem.at[SELF_CHUNK])
                wait(land, CHUNK - CAP, recv_sem.at[SELF_CHUNK])

            @pl.when(a != SELF_CHUNK)
            def _():
                wait(ids_in, CHUNK_MSGS, ids_recv_sem.at[a])
                wait(land, CHUNK, recv_sem.at[a])

            base = pl.multiple_of(a * CHUNK, CHUNK)
            rows = pl.ds(base, CHUNK)
            got = land[rows]
            high = got.astype(BF16)
            unit[rows] = high
            wide = high.astype(F32)
            low = (got - wide).astype(BF16)
            kept = jnp.sum(wide * wide, axis=1, keepdims=True)
            off = jnp.sqrt(jnp.sum(got * got, axis=1, keepdims=True) / jnp.maximum(kept, 1e-30))
            off = jnp.where(kept > 0.0, off - 1.0, 0.0)
            off = jnp.broadcast_to(off, (CHUNK, 128))
            scale_col[rows] = SHARPNESS + SHARPNESS * off
            scale_row[:, rows] = 1.0 + dot_t(hot(iota((8, 128), 1) == 0), off.astype(BF16))
            ids = ids_in[pl.ds(a * CHUNK_MSGS, CHUNK_MSGS), 0, :].astype(BF16)
            in_row = jnp.where(mine, dot(ids, spread), 0.0).astype(BF16)
            row = dot(jnp.ones((8, CHUNK_MSGS), BF16), in_row)
            id_row[:, rows] = row
            at = iota((CHUNK, 128), 0)
            picked = dot(hot(by_48(iota((CHUNK, CHUNK_MSGS), 0)) == iota((CHUNK, CHUNK_MSGS), 1)), ids)
            picked = jnp.where(at - CAP * by_48(at) == iota((CHUNK, 128), 1), picked, 0.0).astype(BF16)
            id_col[rows] = dot(picked, jnp.ones((128, 128), BF16))
            member = hot(iota((CL_OWN, CHUNK), 0).astype(F32) == row[0:1])
            sums[...] += dot(member, high) + dot(member, low)

        def chunk(a, _):
            prepare(a)
            lax.fori_loop(0, a, lambda b, _: (pair(a, b), 0)[1], 0)
            inner(a)
            return 0

        last = CHUNKS - 1
        lax.fori_loop(0, last, chunk, 0)
        prepare(last)
        total = sums[...]
        cen_ref[...] = total * lax.rsqrt(jnp.mean(total * total, axis=1, keepdims=True) + 1e-06)
        for k in range(1, N_GRP):
            pltpu.make_async_remote_copy(
                src_ref=cen_ref, dst_ref=cen_in, send_sem=cen_send_sem.at[k - 1], recv_sem=cen_recv_sem,
                device_id=(lax.rem(grp + k, N_GRP), me), device_id_type=MESH,
            ).start()

        order = messages()

        def give_back(a):
            rows = pl.ds(a * CHUNK, CHUNK)
            part = row_acc[rows]
            high, middle, low = split3(part)
            ones = jnp.ones((8, 128), BF16)
            mass = dot_t(ones, high) + (dot_t(ones, middle) + dot_t(ones, low))
            mass = mass[0:1] + jnp.sum(col_acc[:, rows], axis=0, keepdims=True)
            back = exact(dot_t, jnp.where(mine, mass, 0.0), spread)
            mass_out[pl.ds(a * CHUNK_MSGS, CHUNK_MSGS), 0, :] = back
            for j in range(CHUNK_MSGS):
                i, y_step = order[a * CHUNK_MSGS + j]
                to_grp = lax.rem(grp + N_GRP - y_step, N_GRP)
                to = partner(me, i, back=True)
                here = (i, y_step) == (SELF, 0)

                block = mass_out.at[a * CHUNK_MSGS + j]
                if here:
                    pltpu.make_async_copy(block, mass_in.at[me], local_sem.at[2]).start()
                else:
                    pltpu.make_async_remote_copy(
                        src_ref=block, dst_ref=mass_in.at[me], send_sem=back_send_sem,
                        recv_sem=back_recv_sem, device_id=(to_grp, to), device_id_type=MESH,
                    ).start()

        lax.fori_loop(0, last, lambda b, _: (pair(last, b), 0)[1], 0)
        inner(last)
        for a in range(CHUNKS):
            give_back(a)

        for k in range(1, N_GRP):
            pltpu.make_async_copy(cen_ref, cen_ref, cen_send_sem.at[k - 1]).wait()
        wait(mass_out, MSGS - 1, back_send_sem)
        wait(mass_out, 1, local_sem.at[2])
        wait(mass_in, N_OWN - 1, back_recv_sem)
        lax.fori_loop(0, N_OWN - 1, lambda i, _: (sent(lax.rem(SELF + 1 + i, N_OWN)), 0)[1], 0)
        wait(ids_out, N_OWN - 1, ids_send_sem)

    @pl.when(jnp.logical_not(home))
    def _():
        pltpu.make_async_copy(cen_in, cen_in, cen_recv_sem).wait()
        cen_ref[...] = cen_in[...]
        wait(mass_in, N_OWN, back_recv_sem)

        @pl.when(lax.rem(home_row(me) + grp, 2) == 1)
        def _():
            wait(transit, 16 * CAP, pass_sem)

        wait(ids_out, N_OWN, ids_send_sem)

    got = exact(dot, mass_in[:, 0, :], rank_ref[...])
    mass = jnp.sum(got * rowhot_ref[...], axis=0, keepdims=True)
    score = jnp.broadcast_to(jnp.log(mass) - SHARPNESS, (16, R_DEV))
    dup_ref[...] = exact(dot_t, score, target_ref[...])[0:1].reshape(R_DEV)


def local(embeddings, cluster_ids, owner_map, source_order):
    vmem = pl.BlockSpec(memory_space=pltpu.VMEM)
    dma = pltpu.SemaphoreType.DMA
    dup, centroids = pl.pallas_call(
        kernel,
        out_shape=(jax.ShapeDtypeStruct((R_DEV,), F32), jax.ShapeDtypeStruct((CL_OWN, D), F32)),
        in_specs=[pl.BlockSpec(memory_space=pl.ANY)] + [vmem] * 3,
        out_specs=(vmem, vmem),
        scratch_shapes=[
            pltpu.VMEM((SLOTS, D), F32),
            pltpu.VMEM((N_OWN, 1, 128), F32),
            pltpu.VMEM((MSGS * CAP, D), F32),
            pltpu.VMEM((MSGS, 1, 128), F32),
            pltpu.VMEM((MSGS * CAP, D), BF16),
            pltpu.VMEM((MSGS * CAP, 128), F32),
            pltpu.VMEM((8, MSGS * CAP), F32),
            pltpu.VMEM((MSGS * CAP, 128), F32),
            pltpu.VMEM((8, MSGS * CAP), F32),
            pltpu.VMEM((MSGS * CAP, 128), F32),
            pltpu.VMEM((8, MSGS * CAP), F32),
            pltpu.VMEM((CL_OWN, D), F32),
            pltpu.VMEM((N_OWN, R_DEV), F32),
            pltpu.VMEM((128, R_DEV), BF16),
            pltpu.VMEM((MSGS, 1, 128), F32),
            pltpu.VMEM((N_OWN, 1, 128), F32),
            pltpu.VMEM((CL_OWN, D), F32),
            pltpu.VMEM((16 * CAP, D), F32),
            pltpu.VMEM((R_DEV, D), F32),
            pltpu.VMEM((R_DEV, R_DEV), BF16),
            dma((N_OWN,)), dma((N_OWN,)), dma, dma, dma((CHUNKS,)), dma((CHUNKS,)), dma((3,)), dma, dma, dma((3,)), dma,
        ],
        compiler_params=pltpu.CompilerParams(collective_id=0, has_side_effects=True, vmem_limit_bytes=60 << 20),
        name="owner_gather",
    )(
        embeddings,
        cluster_ids,
        owner_map,
        source_order,
    )
    return dup, centroids


def solution(mesh):
    placed = (P(("grp", "own"), None), P(("grp", "own")), P(), P(("grp", "own")))
    return jax.shard_map(
        local,
        mesh=mesh,
        in_specs=placed,
        out_specs=(P(("grp", "own")), P("own", None)),
        check_vma=False,
    )
```
